256 devices in a mesh: seq: 16 (over z, core), dp: 16 (over x, y).
Axes of the slice: x: 4, y: 4, z: 8, core: 2. Of those that a mesh axis runs over, the one named last changes fastest.
Arguments:
- query_in: bfloat16 [16, 2048, 2048], P('dp', 'seq'), may hold values from -8 to 8
- key_in: bfloat16 [16, 2048, 2048], P('dp', 'seq'), may hold values from -8 to 8
- value_in: bfloat16 [16, 2048, 2048], P('dp', 'seq'), may hold values from -6 to 6
- out_grad: bfloat16 [16, 2048, 2048], P('dp', 'seq'), may hold values from -6 to 6
- out_proj: bfloat16 [2048, 2048], P('seq'), may hold values from -0.125 to 0.125
- key_blocks: int32 [16, 16, 8], P('seq'), may hold values from 0 to 15, as said below
Outputs:
- layer_out: bfloat16 [16, 2048, 2048], P('dp', 'seq')
- query_grad: bfloat16 [16, 2048, 2048], P('dp', 'seq')
- key_grad: bfloat16 [16, 2048, 2048], P('dp', 'seq')
- value_grad: bfloat16 [16, 2048, 2048], P('dp', 'seq')
- proj_grad: float32 [2048, 2048], P('seq')
The draws below stay inside these ranges and needn't reach their ends.
Inputs may be any that keep to these rules, and one draw needn't show every extreme that they name: `key_blocks`: for each head and query block b the 8 listed key blocks are different from one another and include b, b - 1 and b + 1 (modulo 16) and the blocks 0 and 1.
All inputs are finite; a program needn't handle non-finite values.
Results may differ from the reference program's by a relative error of at most 0.02.
Values may be sent and summed in bfloat16 or wider, within the bound.
No kernel may reach another device: no remote copies, remote signals or barrier semaphores. Data moves between devices by JAX's collectives and lax.ppermute only.
A program may use at most 128 MiB of HBM per device.

```python
import math
import jax
import jax.numpy as jnp
from jax import lax

D = 2048
HEADS = 16
HEAD_DIM = 128
BLOCK = 128
SLOTS = 8
SEQ_LEN = 2048
SEQS = 16
INNER = 2048
BLOCKS = 16


def draw_query_in(key, part):
    full_shape = (SEQS, SEQ_LEN, HEADS * HEAD_DIM)
    inner_key = jax.random.fold_in(key, 11)
    drawn = jnp.clip(jax.random.normal(inner_key, full_shape, jnp.float32), -4.0, 4.0) * 1.5
    return drawn.astype(jnp.bfloat16)


def draw_key_in(key, part):
    full_shape = (SEQS, SEQ_LEN, HEADS * HEAD_DIM)
    inner_key = jax.random.fold_in(key, 21)
    drawn = jnp.clip(jax.random.normal(inner_key, full_shape, jnp.float32), -4.0, 4.0)
    return drawn.astype(jnp.bfloat16)


def draw_key_blocks(key, part):
    row_total = HEADS * BLOCKS
    row_keys = jax.random.split(jax.random.fold_in(key, 31), row_total)
    ranking = jax.vmap(lambda one_key: jax.random.permutation(one_key, BLOCKS))(row_keys).astype(jnp.int32)
    own_block = (jnp.arange(row_total, dtype=jnp.int32) % BLOCKS)[:, None]
    column = jnp.arange(BLOCKS, dtype=jnp.int32)[None, :]
    needed = (column == own_block) | (column == (own_block + 1) % BLOCKS) | (column == (own_block + BLOCKS - 1) % BLOCKS) | (column <= 1)
    priority = ranking + needed.astype(jnp.int32) * BLOCKS
    chosen = lax.top_k(priority, SLOTS)[1]
    return chosen.reshape(HEADS, BLOCKS, SLOTS).astype(jnp.int32)


def level_of(rng, extent, shards, least, top_value):
    level = 1.0
    for dim, shards_of in shards:
        heights = jax.random.uniform(jax.random.fold_in(jax.random.fold_in(rng, 6), dim), (shards_of,), jnp.float32, least / len(shards), top_value / len(shards))
        level = level * jnp.repeat(jnp.exp(heights), extent[dim] // shards_of).reshape((-1,) + (1,) * (len(extent) - 1 - dim))
    return level


def centred(rng, dims, scale, bound, cuts=(), kind=jnp.bfloat16):
    result = jax.random.normal(rng, dims, jnp.float32) * scale
    if len(cuts) > 0:
        result = level_of(rng, dims, cuts, -0.22, 0.18) * result
    return jnp.clip(result, min=-bound, max=bound).astype(kind)


def setup_inputs(seed: int = 0) -> dict:
    keys = jax.random.split(jax.random.key(seed), 7)
    query_in = draw_query_in(jax.random.fold_in(keys[6], 71), 0)
    key_in = draw_key_in(jax.random.fold_in(keys[6], 71), 0)
    value_in = centred(keys[2], (SEQS, SEQ_LEN, INNER), 1.0, 6.0, ((0, 16), (1, 16)))
    out_grad = centred(keys[3], (SEQS, SEQ_LEN, D), 1.0, 6.0, ((0, 16), (1, 16)))
    out_proj = centred(keys[4], (INNER, D), INNER ** -0.5, 0.125, ((0, 16),))
    key_blocks = draw_key_blocks(jax.random.fold_in(keys[6], 71), 0)
    return {"query_in": query_in, "key_in": key_in, "value_in": value_in, "out_grad": out_grad, "out_proj": out_proj, "key_blocks": key_blocks}


def head_forward(q_one, k_one, v_one, blocks):
    block_count = blocks.shape[0]
    inv_root = 1.0 / math.sqrt(HEAD_DIM)
    q_blocks = q_one.reshape(block_count, BLOCK, HEAD_DIM).astype(jnp.float32)
    k_picked = k_one.reshape(block_count, BLOCK, HEAD_DIM)[blocks].astype(jnp.float32)
    v_picked = v_one.reshape(block_count, BLOCK, HEAD_DIM)[blocks].astype(jnp.float32)
    scores = jnp.einsum('qid,qsjd->qisj', q_blocks, k_picked) * inv_root
    row_max = lax.optimization_barrier(jnp.max(scores, axis=(2, 3), keepdims=True))
    log_total = row_max + jnp.log(lax.optimization_barrier(jnp.sum(jnp.exp(scores - row_max), axis=(2, 3), keepdims=True)))
    prob_bf = jnp.exp(scores - log_total).astype(jnp.bfloat16)
    attended = jnp.einsum('qisj,qsjd->qid', prob_bf.astype(jnp.float32), v_picked)
    return (attended.astype(jnp.bfloat16).reshape(block_count * BLOCK, HEAD_DIM), log_total)

def head_backward(q_one, k_one, v_one, blocks, attended, d_attended, log_total):
    block_count, slot_count = blocks.shape
    inv_root = 1.0 / math.sqrt(HEAD_DIM)
    q_blocks = q_one.reshape(block_count, BLOCK, HEAD_DIM).astype(jnp.float32)
    k_picked = k_one.reshape(block_count, BLOCK, HEAD_DIM)[blocks].astype(jnp.float32)
    v_picked = v_one.reshape(block_count, BLOCK, HEAD_DIM)[blocks].astype(jnp.float32)
    scores = jnp.einsum('qid,qsjd->qisj', q_blocks, k_picked) * inv_root
    exact_prob = jnp.exp(scores - log_total)
    prob_bf = exact_prob.astype(jnp.bfloat16)
    d_blocks = d_attended.reshape(block_count, BLOCK, HEAD_DIM).astype(jnp.float32)
    a_blocks = attended.reshape(block_count, BLOCK, HEAD_DIM).astype(jnp.float32)
    row_dot = lax.optimization_barrier(jnp.sum(d_blocks * a_blocks, axis=-1))[:, :, None, None]
    prob_grad = jnp.einsum('qid,qsjd->qisj', d_blocks, v_picked)
    score_grad = (exact_prob * (prob_grad - row_dot) * inv_root).astype(jnp.bfloat16)
    score_float = score_grad.astype(jnp.float32)
    q_grad = jnp.einsum('qisj,qsjd->qid', score_float, k_picked)
    k_parts = jnp.einsum('qisj,qid->qsjd', score_float, q_blocks).reshape(block_count * slot_count, BLOCK * HEAD_DIM)
    v_parts = jnp.einsum('qisj,qid->qsjd', prob_bf.astype(jnp.float32), d_blocks).reshape(block_count * slot_count, BLOCK * HEAD_DIM)
    owners = blocks.reshape(-1)
    k_grad = jax.ops.segment_sum(k_parts, owners, num_segments=block_count)
    v_grad = jax.ops.segment_sum(v_parts, owners, num_segments=block_count)
    length = block_count * BLOCK
    return (q_grad.astype(jnp.bfloat16).reshape(length, HEAD_DIM), k_grad.astype(jnp.bfloat16).reshape(length, HEAD_DIM), v_grad.astype(jnp.bfloat16).reshape(length, HEAD_DIM))

def reference(query_in, key_in, value_in, out_grad, out_proj, key_blocks):
    seq_count, length, inner_width = query_in.shape
    head_count = inner_width // HEAD_DIM

    def to_heads(matrix):
        return matrix.reshape(length, head_count, HEAD_DIM).transpose(1, 0, 2)

    def from_heads(stacked):
        return stacked.transpose(1, 0, 2).reshape(length, inner_width)

    def one_seq(wgrad_acc, seq_items):
        q_seq, k_seq, v_seq, d_seq = seq_items
        q_heads, k_heads, v_heads = (to_heads(q_seq), to_heads(k_seq), to_heads(v_seq))
        attended, log_total = lax.map(lambda packed: head_forward(*packed), (q_heads, k_heads, v_heads, key_blocks))
        attn = from_heads(attended)
        layer_seq = jnp.dot(attn, out_proj, preferred_element_type=jnp.float32).astype(jnp.bfloat16)
        attn_grad = jnp.dot(d_seq, out_proj.T, preferred_element_type=jnp.float32).astype(jnp.bfloat16)
        wgrad_acc = wgrad_acc + jnp.dot(attn.T, d_seq, preferred_element_type=jnp.float32)
        q_grad, k_grad, v_grad = lax.map(lambda packed: head_backward(*packed), (q_heads, k_heads, v_heads, key_blocks, attended, to_heads(attn_grad), log_total))
        return (wgrad_acc, (layer_seq, from_heads(q_grad), from_heads(k_grad), from_heads(v_grad)))
    start_acc = jnp.zeros((inner_width, out_proj.shape[1]), jnp.float32)
    summed, (layer_out, query_grad, key_grad, value_grad) = lax.scan(one_seq, start_acc, (query_in, key_in, value_in, out_grad))
    proj_grad = summed * (1.0 / math.sqrt(seq_count * length))
    return (layer_out, query_grad, key_grad, value_grad, proj_grad)
```

```python
import functools
import math

import jax
import jax.numpy as jnp
from jax import lax
from jax.experimental import pallas as pl
from jax.experimental.pallas import tpu as pltpu
from jax.sharding import Mesh
from jax.sharding import PartitionSpec as P

HEAD_DIM = 128
BLOCK = 128
INV_ROOT = 1.0 / math.sqrt(HEAD_DIM)
LOG2E = 1.0 / math.log(2.0)
BF16 = jnp.bfloat16
F32 = jnp.float32


def column_blocks(ref_value, count):
    return [ref_value[:, j * BLOCK : (j + 1) * BLOCK] for j in range(count)]


def pack_kernel(chunk_ref, q_ref, k_ref, v_ref, g_ref, w_ref, qkv_ref, gw_ref):
    count = qkv_ref.shape[0]
    for j in range(count):
        cols = slice(j * BLOCK, (j + 1) * BLOCK)
        qkv_ref[j, 0] = q_ref[:, cols]
        qkv_ref[j, 1] = k_ref[:, cols]
        qkv_ref[j, 2] = v_ref[:, cols]
        gw_ref[j] = g_ref[:, cols]
    gw_ref[count] = w_ref[:, pl.ds(pl.multiple_of(chunk_ref[0] * BLOCK, BLOCK), BLOCK)]


def pack(chunk, q, k, v, g, w):
    count = q.shape[1] // BLOCK
    vm = pl.BlockSpec(memory_space=pltpu.VMEM)
    return pl.pallas_call(
        pack_kernel,
        out_shape=(
            jax.ShapeDtypeStruct((count, 3, BLOCK, BLOCK), BF16),
            jax.ShapeDtypeStruct((count + 1, BLOCK, BLOCK), BF16),
        ),
        in_specs=[pl.BlockSpec(memory_space=pltpu.SMEM)] + [vm] * 5,
        out_specs=(vm, vm),
        compiler_params=pltpu.CompilerParams(vmem_limit_bytes=24 * 1024 * 1024),
        name="pack",
    )(chunk, q, k, v, g, w)


def attention_kernel(
    blocks_ref, core_ref, qkv_ref, own_ref, other_ref, w_ref, out_ref, pg_ref,
    kv_ref, kt_ref, vt_ref, acc_ref, wt_ref, pg_acc_ref,
):
    step = pl.program_id(0)
    block_count, slot_count = blocks_ref.shape
    half = block_count // 2
    zero = jnp.zeros((BLOCK, HEAD_DIM), BF16)

    @pl.when(step == 0)
    def _():
        def prepare(c, carry):
            rows = pl.ds(pl.multiple_of(c * BLOCK, BLOCK), BLOCK)
            k_one, v_one = qkv_ref[c, 1], qkv_ref[c, 2]
            kv_ref[rows, :] = jnp.concatenate([k_one, v_one], axis=1)
            kt_ref[c] = k_one.T
            vt_ref[c] = v_one.T
            acc_ref[rows, :] = jnp.zeros((BLOCK, 2 * HEAD_DIM), F32)
            return carry

        lax.fori_loop(0, block_count, prepare, 0)
        wt_ref[...] = w_ref[...].T
        pg_acc_ref[...] = jnp.zeros_like(pg_acc_ref)

    def work(g_ref, b):
        g_one = jnp.concatenate([g_ref[0, j] for j in range(block_count)], axis=1)
        d_one = jnp.dot(g_one, wt_ref[...], preferred_element_type=F32).astype(BF16)
        q_one = qkv_ref[b, 0]
        q_t, d_t = q_one.T, d_one.T
        owners = [blocks_ref[b, s] for s in range(slot_count)]
        picks = [pl.ds(pl.multiple_of(c * BLOCK, BLOCK), BLOCK) for c in owners]
        right = jnp.concatenate(
            [jnp.concatenate([q_t, zero], axis=1), jnp.concatenate([zero, d_t], axis=1)], axis=0
        )
        kv = jnp.concatenate([kv_ref[p, :] for p in picks], axis=0)
        both = jnp.dot(kv, right, preferred_element_type=F32)
        scores, prob_grad = both[:, :BLOCK], both[:, BLOCK:]
        top = jnp.max(scores, axis=0, keepdims=True)
        raised = jnp.exp2((scores - top) * (INV_ROOT * LOG2E))
        prob = raised * (1.0 / jnp.sum(raised, axis=0, keepdims=True))
        prob_bf = prob.astype(BF16)
        v_t = jnp.concatenate([vt_ref[c] for c in owners], axis=1)
        attn_t = jnp.dot(v_t, prob_bf, preferred_element_type=F32).astype(BF16)
        row_dot = jnp.sum(attn_t.astype(F32) * d_t.astype(F32), axis=0, keepdims=True)
        score_grad = (prob * (prob_grad - row_dot) * INV_ROOT).astype(BF16)
        k_t = jnp.concatenate([kt_ref[c] for c in owners], axis=1)
        dq_t = jnp.dot(k_t, score_grad, preferred_element_type=F32)
        out_ref[b, 0] = attn_t.T
        out_ref[b, 1] = dq_t.astype(BF16).T
        pg_acc_ref[...] += jnp.dot(attn_t, g_one, preferred_element_type=F32)
        back = jnp.concatenate(
            [jnp.concatenate([q_one, zero], axis=1), jnp.concatenate([zero, d_one], axis=1)], axis=0
        )
        parts = jnp.dot(
            jnp.concatenate([score_grad, prob_bf], axis=1), back, preferred_element_type=F32
        )
        for s, p in enumerate(picks):
            acc_ref[p, :] += parts[s * BLOCK : (s + 1) * BLOCK, :]

    @pl.when(step < half)
    def _():
        work(own_ref, 2 * step + core_ref[0])

    @pl.when(step >= half)
    def _():
        work(other_ref, 2 * (step - half) + 1 - core_ref[0])

    @pl.when(step == block_count - 1)
    def _():
        def finish(c, carry):
            rows = pl.ds(pl.multiple_of(c * BLOCK, BLOCK), BLOCK)
            out_ref[c, 2] = acc_ref[rows, :HEAD_DIM].astype(BF16)
            out_ref[c, 3] = acc_ref[rows, HEAD_DIM:].astype(BF16)
            return carry

        lax.fori_loop(0, block_count, finish, 0)
        for j in range(block_count):
            pg_ref[j] = pg_acc_ref[:, j * BLOCK : (j + 1) * BLOCK].astype(BF16)


def attention(blocks, core, qkv, own, other, w):
    count = qkv.shape[0]
    half = count // 2
    width = w.shape[1]
    chunks = width // BLOCK
    vm = pl.BlockSpec(memory_space=pltpu.VMEM)
    sm = pl.BlockSpec(memory_space=pltpu.SMEM)
    g_block = (1, chunks, BLOCK, BLOCK)
    return pl.pallas_call(
        attention_kernel,
        grid=(count,),
        out_shape=(
            jax.ShapeDtypeStruct((count, 4, BLOCK, HEAD_DIM), BF16),
            jax.ShapeDtypeStruct((chunks, HEAD_DIM, BLOCK), BF16),
        ),
        in_specs=[
            sm,
            sm,
            vm,
            pl.BlockSpec(g_block, lambda i: (jnp.minimum(i, half - 1), 0, 0, 0)),
            pl.BlockSpec(g_block, lambda i: (jnp.maximum(i - half, 0), 0, 0, 0)),
            vm,
        ],
        out_specs=(vm, vm),
        scratch_shapes=[
            pltpu.VMEM((count * BLOCK, 2 * HEAD_DIM), BF16),
            pltpu.VMEM((count, HEAD_DIM, BLOCK), BF16),
            pltpu.VMEM((count, HEAD_DIM, BLOCK), BF16),
            pltpu.VMEM((count * BLOCK, 2 * HEAD_DIM), F32),
            pltpu.VMEM((width, HEAD_DIM), BF16),
            pltpu.VMEM((HEAD_DIM, width), F32),
        ],
        compiler_params=pltpu.CompilerParams(
            dimension_semantics=("arbitrary",), vmem_limit_bytes=40 * 1024 * 1024
        ),
        name="attention",
    )(blocks, core, qkv, own, other, w)


def project_kernel(mine_ref, w_ref, layer_ref, dq_ref, dk_ref, dv_ref, rows_ref):
    count = mine_ref.shape[0]

    @pl.when(pl.program_id(0) == 0)
    def _():
        for h in range(count):
            cols = slice(h * HEAD_DIM, (h + 1) * HEAD_DIM)
            rows_ref[:, cols] = mine_ref[h, 0]
            dq_ref[:, cols] = mine_ref[h, 1]
            dk_ref[:, cols] = mine_ref[h, 2]
            dv_ref[:, cols] = mine_ref[h, 3]

    weights = jnp.concatenate(
        [w_ref[d].reshape(count * HEAD_DIM, BLOCK) for d in range(w_ref.shape[0])], axis=1
    )
    layer_ref[...] = jnp.dot(rows_ref[...], weights, preferred_element_type=F32).astype(BF16)


def project(mine, w):
    heads = mine.shape[0]
    chunks = w.shape[0]
    together = 4
    vm = pl.BlockSpec(memory_space=pltpu.VMEM)
    wide = jax.ShapeDtypeStruct((BLOCK, heads * HEAD_DIM), BF16)
    return pl.pallas_call(
        project_kernel,
        grid=(chunks // together,),
        out_shape=(jax.ShapeDtypeStruct((BLOCK, chunks * BLOCK), BF16), wide, wide, wide),
        in_specs=[
            vm,
            pl.BlockSpec((together, heads, HEAD_DIM, BLOCK), lambda i: (i, 0, 0, 0)),
        ],
        out_specs=(pl.BlockSpec((BLOCK, together * BLOCK), lambda i: (0, i)), vm, vm, vm),
        scratch_shapes=[pltpu.VMEM((BLOCK, heads * HEAD_DIM), BF16)],
        compiler_params=pltpu.CompilerParams(
            dimension_semantics=("arbitrary",), vmem_limit_bytes=40 * 1024 * 1024
        ),
        name="project",
    )(mine, w)


def body(query_in, key_in, value_in, out_grad, out_proj, key_blocks):
    seq, dp = ("z", "c"), ("x", "y")
    core = lax.axis_index("c")
    tokens = lax.axis_size(seq) * lax.axis_size(dp) * query_in.shape[1]
    place = lax.axis_index(dp).astype(jnp.int32)[None]
    qkv_out, gw = pack(place, query_in[0], key_in[0], value_in[0], out_grad[0], out_proj)
    gw_own = lax.all_gather(gw, "z", axis=0)
    qkv = lax.all_to_all(qkv_out, seq, split_axis=0, concat_axis=0, tiled=True)
    gw_other = lax.ppermute(gw_own, "c", [(0, 1), (1, 0)])
    w_own, w_other = gw_own[:, -1], gw_other[:, -1]
    first, second = jnp.where(core == 0, w_own, w_other), jnp.where(core == 0, w_other, w_own)
    w_chunk = jnp.stack([first, second], axis=1).reshape((-1,) + w_own.shape[1:])
    w_all = lax.all_gather(w_chunk, dp, axis=0)
    out, pg = attention(
        key_blocks[0], core.astype(jnp.int32)[None], qkv, gw_own, gw_other, out_proj
    )
    mine = lax.all_to_all(out, seq, split_axis=0, concat_axis=0, tiled=True)
    pg_parts = lax.all_to_all(pg, dp, split_axis=0, concat_axis=0, tiled=True)
    pg_sum = (jnp.sum(pg_parts.astype(F32), axis=0) * (1.0 / math.sqrt(tokens))).astype(BF16)
    pg_all = lax.all_to_all(
        jnp.broadcast_to(pg_sum[None], pg.shape), dp, split_axis=0, concat_axis=0, tiled=True
    )
    proj_grad = pg_all.transpose(1, 0, 2).reshape(out_proj.shape).astype(F32)
    layer, dq, dk, dv = project(mine, w_all)
    return layer[None], dq[None], dk[None], dv[None], proj_grad


def solution(mesh):
    split = Mesh(mesh.devices.reshape(8, 2, 4, 4), ("z", "c", "x", "y"))
    rows = P(("x", "y"), ("z", "c"), None)
    in_specs = (rows, rows, rows, rows, P(("z", "c"), None), P(("z", "c"), None, None))
    out_specs = (rows, rows, rows, rows, P(("z", "c"), None))
    return jax.shard_map(body, mesh=split, in_specs=in_specs, out_specs=out_specs, check_vma=False)
```

```python
import functools
import math

import jax
import jax.numpy as jnp
from jax import lax
from jax.experimental import pallas as pl
from jax.experimental.pallas import tpu as pltpu
from jax.sharding import Mesh
from jax.sharding import PartitionSpec as P

HEAD_DIM = 128
BLOCK = 128
INV_ROOT = 1.0 / math.sqrt(HEAD_DIM)
LOG2E = 1.0 / math.log(2.0)
BF16 = jnp.bfloat16
F32 = jnp.float32
VM = pl.BlockSpec(memory_space=pltpu.VMEM)
SM = pl.BlockSpec(memory_space=pltpu.SMEM)
ANY = pl.BlockSpec(memory_space=pl.ANY)
MIB = 1024 * 1024


def like(*shape, dtype=BF16):
    return jax.ShapeDtypeStruct(shape, dtype)


def pack_kernel(place_ref, q_ref, k_ref, v_ref, g_ref, w_ref, qkv_ref, gw_ref, sem):
    count = qkv_ref.shape[0]
    copies = []

    def send(source, target):
        copy = pltpu.make_async_copy(source, target, sem.at[len(copies)])
        copy.start()
        copies.append(copy)

    send(w_ref.at[:, pl.ds(pl.multiple_of(place_ref[0] * BLOCK, BLOCK), BLOCK)], gw_ref.at[count])
    for j in range(count):
        cols = pl.ds(j * BLOCK, BLOCK)
        send(g_ref.at[:, cols], gw_ref.at[j])
        send(q_ref.at[:, cols], qkv_ref.at[j, 0])
        send(k_ref.at[:, cols], qkv_ref.at[j, 1])
        send(v_ref.at[:, cols], qkv_ref.at[j, 2])
    for copy in copies:
        copy.wait()


def pack(place, q, k, v, g, w):
    count = q.shape[1] // BLOCK
    return pl.pallas_call(
        pack_kernel,
        out_shape=(like(count, 3, BLOCK, BLOCK), like(count + 1, BLOCK, BLOCK)),
        in_specs=[SM] + [ANY] * 5,
        out_specs=(ANY, ANY),
        scratch_shapes=[pltpu.SemaphoreType.DMA((4 * count + 1,))],
        name="pack",
    )(place, q, k, v, g, w)


def rows_of(c):
    return pl.ds(pl.multiple_of(c * BLOCK, BLOCK), BLOCK)


def forward_kernel(blocks_ref, qkv_ref, attn_ref, attn_t_ref, lse_ref, vt_ref):
    block_count, slot_count = blocks_ref.shape

    def prepare(c, carry):
        vt_ref[c] = qkv_ref[c, 2].T
        return carry

    lax.fori_loop(0, block_count, prepare, 0, unroll=4)

    def one(b):
        owners = [blocks_ref[b, s] for s in range(slot_count)]
        keys = jnp.concatenate([qkv_ref[c, 1] for c in owners], axis=0)
        scores = jnp.dot(keys, qkv_ref[b, 0].T, preferred_element_type=F32)
        top = jnp.max(scores, axis=0, keepdims=True)
        raised = jnp.exp2((scores - top) * (INV_ROOT * LOG2E))
        total = jnp.sum(raised, axis=0, keepdims=True)
        prob = (raised * (1.0 / total)).astype(BF16)
        v_t = jnp.concatenate([vt_ref[c] for c in owners], axis=1)
        attn_t = jnp.dot(v_t, prob, preferred_element_type=F32).astype(BF16)
        attn_t_ref[b] = attn_t
        attn_ref[b] = attn_t.T
        lse_ref[b] = top * (INV_ROOT * LOG2E) + jnp.log2(total)

    def step(i, carry):
        one(2 * i)
        one(2 * i + 1)
        return carry

    lax.fori_loop(0, block_count // 2, step, 0)


def forward(blocks, qkv):
    count = qkv.shape[0]
    return pl.pallas_call(
        forward_kernel,
        out_shape=(
            like(count, BLOCK, HEAD_DIM),
            like(count, HEAD_DIM, BLOCK),
            like(count, 1, BLOCK, dtype=F32),
        ),
        in_specs=[SM, VM],
        out_specs=(VM, VM, VM),
        scratch_shapes=[pltpu.VMEM((count, HEAD_DIM, BLOCK), BF16)],
        compiler_params=pltpu.CompilerParams(vmem_limit_bytes=24 * MIB),
        name="forward",
    )(blocks, qkv)


def backward_kernel(parts, blocks_ref, place_ref, qkv_ref, attn_t_ref, lse_ref, w_ref, *refs):
    g_refs = refs[: len(parts)]
    out_ref, pg_ref, kv_ref, kt_ref, acc_ref, wt_ref, pg_acc_ref, g_buf, sem = refs[len(parts) :]
    block_count, slot_count = blocks_ref.shape
    half = block_count // 2
    zero = jnp.zeros((BLOCK, HEAD_DIM), BF16)

    def fetch(pair, act):
        for n, (shift, side, low, high) in enumerate(parts):
            if isinstance(pair, int) and pair != shift:
                continue

            def go(n=n, shift=shift, side=side, low=low, high=high):
                slot = shift % 2
                act(
                    pltpu.make_async_copy(
                        g_refs[n].at[pl.ds(0, high - low)],
                        g_buf.at[slot, side, pl.ds(low, high - low)],
                        sem.at[slot, side, 0 if low == 0 else 1],
                    )
                )

            if isinstance(pair, int):
                go()
            else:
                pl.when(pair == shift)(go)

    fetch(0, lambda copy: copy.start())

    def prepare(c, carry):
        k_one, v_one = qkv_ref[c, 1], qkv_ref[c, 2]
        kv_ref[rows_of(c), :] = jnp.concatenate([k_one, v_one], axis=1)
        kt_ref[c] = k_one.T
        acc_ref[rows_of(c), :] = jnp.zeros((BLOCK, 2 * HEAD_DIM), F32)
        return carry

    lax.fori_loop(0, block_count, prepare, 0, unroll=2)
    wt_ref[...] = w_ref[...].T
    pg_acc_ref[...] = jnp.zeros_like(pg_acc_ref)

    def one(b, d_one):
        q_one = qkv_ref[b, 0]
        q_t, d_t = q_one.T, d_one.T
        owners = [blocks_ref[b, s] for s in range(slot_count)]
        right = jnp.concatenate(
            [jnp.concatenate([q_t, zero], axis=1), jnp.concatenate([zero, d_t], axis=1)], axis=0
        )
        kv = jnp.concatenate([kv_ref[rows_of(c), :] for c in owners], axis=0)
        both = jnp.dot(kv, right, preferred_element_type=F32)
        scores, prob_grad = both[:, :BLOCK], both[:, BLOCK:]
        prob = jnp.exp2(scores * (INV_ROOT * LOG2E) - lse_ref[b])
        row_dot = jnp.sum(attn_t_ref[b].astype(F32) * d_t.astype(F32), axis=0, keepdims=True)
        score_grad = (prob * (prob_grad - row_dot) * INV_ROOT).astype(BF16)
        k_t = jnp.concatenate([kt_ref[c] for c in owners], axis=1)
        dq_t = jnp.dot(k_t, score_grad, preferred_element_type=F32)
        out_ref[b, 0] = dq_t.astype(BF16).T
        back = jnp.concatenate(
            [jnp.concatenate([q_one, zero], axis=1), jnp.concatenate([zero, d_one], axis=1)], axis=0
        )
        return owners, jnp.dot(
            jnp.concatenate([score_grad, prob.astype(BF16)], axis=1),
            back,
            preferred_element_type=F32,
        )

    def step(i, carry):
        slot = lax.rem(i, 2)
        fetch(i, lambda copy: copy.wait())
        fetch(i + 1, lambda copy: copy.start())
        chip = lax.rem(place_ref[0] + place_ref[2 + i], half)
        mine = 2 * chip + place_ref[1]
        theirs = 2 * chip + 1 - place_ref[1]
        g_two = jnp.concatenate(
            [
                jnp.concatenate([g_buf[slot, side, j] for j in range(pg_ref.shape[0])], axis=1)
                for side in range(2)
            ],
            axis=0,
        )
        d_two = jnp.dot(g_two, wt_ref[...], preferred_element_type=F32).astype(BF16)
        results = [one(mine, d_two[:BLOCK]), one(theirs, d_two[BLOCK:])]
        for owners, found in results:
            for s, c in enumerate(owners):
                acc_ref[rows_of(c), :] += found[s * BLOCK : (s + 1) * BLOCK, :]
        attn_two = jnp.concatenate([attn_t_ref[mine], attn_t_ref[theirs]], axis=1)
        pg_acc_ref[...] += jnp.dot(attn_two, g_two, preferred_element_type=F32)
        return carry

    lax.fori_loop(0, half, step, 0)

    def finish(c, carry):
        out_ref[c, 1] = acc_ref[rows_of(c), :HEAD_DIM].astype(BF16)
        out_ref[c, 2] = acc_ref[rows_of(c), HEAD_DIM:].astype(BF16)
        return carry

    lax.fori_loop(0, block_count, finish, 0, unroll=2)
    for j in range(pg_ref.shape[0]):
        pg_ref[j] = pg_acc_ref[:, j * BLOCK : (j + 1) * BLOCK].astype(BF16)


def backward(blocks, place, qkv, attn_t, lse, w, parts, shards):
    count = qkv.shape[0]
    width = w.shape[1]
    chunks = width // BLOCK
    return pl.pallas_call(
        functools.partial(backward_kernel, parts),
        out_shape=(like(count, 3, BLOCK, HEAD_DIM), like(chunks, HEAD_DIM, BLOCK)),
        in_specs=[SM, SM] + [VM] * 4 + [ANY] * len(shards),
        out_specs=(VM, VM),
        scratch_shapes=[
            pltpu.VMEM((count * BLOCK, 2 * HEAD_DIM), BF16),
            pltpu.VMEM((count, HEAD_DIM, BLOCK), BF16),
            pltpu.VMEM((count * BLOCK, 2 * HEAD_DIM), F32),
            pltpu.VMEM((width, HEAD_DIM), BF16),
            pltpu.VMEM((HEAD_DIM, width), F32),
            pltpu.VMEM((2, 2, chunks, BLOCK, BLOCK), BF16),
            pltpu.SemaphoreType.DMA((2, 2, 2)),
        ],
        compiler_params=pltpu.CompilerParams(vmem_limit_bytes=32 * MIB),
        name="backward",
    )(blocks, place, qkv, attn_t, lse, w, *shards)


def project_kernel(groups, heads_ref, cols_ref, mine_ref, *refs):
    w_refs, layer_ref, rows_ref = refs[:-2], refs[-2], refs[-1]
    count = mine_ref.shape[0]
    for e in range(count):
        rows_ref[:, e * HEAD_DIM : (e + 1) * HEAD_DIM] = mine_ref[heads_ref[e]]
    half = count // 2
    rows = rows_ref[...]
    for i in range(groups):
        for j in range(0, groups, 2):
            weights = jnp.concatenate(
                [
                    jnp.concatenate(
                        [
                            w_refs[i][t].reshape(half * HEAD_DIM, BLOCK),
                            w_refs[groups + t][i].reshape(half * HEAD_DIM, BLOCK),
                        ],
                        axis=0,
                    )
                    for t in (j, j + 1)
                ],
                axis=1,
            )
            found = jnp.dot(rows, weights, preferred_element_type=F32).astype(BF16)
            for n in range(2):
                at = pl.multiple_of(cols_ref[i * groups + j + n] * BLOCK, BLOCK)
                layer_ref[:, pl.ds(at, BLOCK)] = found[:, n * BLOCK : (n + 1) * BLOCK]


def project(heads, cols, mine, pieces):
    count = mine.shape[0]
    groups = len(pieces) // 2
    return pl.pallas_call(
        functools.partial(project_kernel, groups),
        out_shape=like(BLOCK, groups * groups * BLOCK),
        in_specs=[SM, SM, VM] + [VM] * len(pieces),
        out_specs=VM,
        scratch_shapes=[pltpu.VMEM((BLOCK, count * HEAD_DIM), BF16)],
        compiler_params=pltpu.CompilerParams(vmem_limit_bytes=32 * MIB),
        name="project",
    )(heads, cols, mine, *pieces)


def unpack_kernel(cols_ref, grads_ref, *refs):
    pg_refs = refs[:-4]
    dq_ref, dk_ref, dv_ref, pg_ref = refs[-4:]
    for h in range(grads_ref.shape[0]):
        cols = slice(h * HEAD_DIM, (h + 1) * HEAD_DIM)
        dq_ref[:, cols] = grads_ref[h, 0]
        dk_ref[:, cols] = grads_ref[h, 1]
        dv_ref[:, cols] = grads_ref[h, 2]
    groups = len(pg_refs)
    for i in range(groups):
        for j in range(groups):
            at = pl.multiple_of(cols_ref[i * groups + j] * BLOCK, BLOCK)
            pg_ref[:, pl.ds(at, BLOCK)] = pg_refs[i][j].astype(F32)


def unpack(cols, grads, pg_pieces):
    wide = like(BLOCK, grads.shape[0] * HEAD_DIM)
    groups = len(pg_pieces)
    return pl.pallas_call(
        unpack_kernel,
        out_shape=(wide, wide, wide, like(HEAD_DIM, groups * groups * BLOCK, dtype=F32)),
        in_specs=[SM, VM] + [VM] * groups,
        out_specs=(VM,) * 4,
        compiler_params=pltpu.CompilerParams(vmem_limit_bytes=24 * MIB),
        name="unpack",
    )(cols, grads, *pg_pieces)


def shifted(value, axis, by):
    size = lax.axis_size(axis)
    return lax.ppermute(value, axis, [(i, (i + by) % size) for i in range(size)])


def from_others(value, axis):
    return [value] + [shifted(value, axis, i) for i in range(1, lax.axis_size(axis))]


def spread(value, axis):
    size = lax.axis_size(axis)
    here = lax.axis_index(axis)
    total = lax.dynamic_index_in_dim(value, here, 0, keepdims=False).astype(F32)
    for i in range(1, size):
        piece = lax.dynamic_index_in_dim(value, (here + i) % size, 0, keepdims=False)
        total = total + shifted(piece, axis, i).astype(F32)
    return total


def ring(gw):
    size = lax.axis_size("z")
    found = [(0, 0, gw.shape[0], gw)]
    up = down = gw
    for k in range(1, size // 2):
        up, down = shifted(up, "z", 1), shifted(down, "z", -1)
        found += [(-k, 0, gw.shape[0], up), (k, 0, gw.shape[0], down)]
    cut = gw.shape[0] // 2
    found.append((size // 2, 0, cut, shifted(up[:cut], "z", 1)))
    found.append((size // 2, cut, gw.shape[0], shifted(down[cut:], "z", -1)))
    return found


def body(query_in, key_in, value_in, out_grad, out_proj, key_blocks):
    seq, dp = ("z", "c"), ("x", "y")
    chips = lax.axis_size("z")
    core, z = lax.axis_index("c").astype(jnp.int32), lax.axis_index("z").astype(jnp.int32)
    x, y = lax.axis_index("x").astype(jnp.int32), lax.axis_index("y").astype(jnp.int32)
    tokens = lax.axis_size(seq) * lax.axis_size(dp) * query_in.shape[1]
    groups = lax.axis_size("x")
    place = (x * groups + y)[None]
    qkv_out, gw = pack(place, query_in[0], key_in[0], value_in[0], out_grad[0], out_proj)
    qkv = lax.all_to_all(qkv_out, seq, split_axis=0, concat_axis=0, tiled=True)
    last = gw.shape[0] - 1

    shifts = []
    parts, shards, w_blocks, heads = [], [], [], []
    for shift, low, high, array in ring(gw):
        if shift not in shifts:
            shifts.append(shift)
        pair = shifts.index(shift)
        other = lax.ppermute(array, "c", [(0, 1), (1, 0)])
        for side, piece in enumerate((array, other)):
            parts.append((pair, side, low, min(high, last)))
            shards.append(piece)
            if high == last + 1:
                w_blocks.append(piece[last - low])
                owner = 2 * ((z + shift) % chips)
                heads.append(owner + (core if side == 0 else 1 - core))
    heads = jnp.stack(heads)
    w_low, w_high = jnp.stack(w_blocks[: chips]), jnp.stack(w_blocks[chips:])
    w_pieces = from_others(jnp.stack(from_others(w_low, "y")), "x")
    w_pieces += from_others(jnp.stack(from_others(w_high, "x")), "y")
    index = jnp.arange(groups, dtype=jnp.int32)
    cols = (((x - index) % groups)[:, None] * groups + ((y - index) % groups)[None]).reshape(-1)

    blocks = key_blocks[0]
    attn, attn_t, lse = forward(blocks, qkv)
    attn_rows = lax.all_to_all(attn, seq, split_axis=0, concat_axis=0, tiled=True)
    spot = jnp.stack([z, core] + [jnp.int32(s % chips) for s in shifts])
    grads, pg = backward(blocks, spot, qkv, attn_t, lse, out_proj, tuple(parts), shards)
    grad_rows = lax.all_to_all(grads, seq, split_axis=0, concat_axis=0, tiled=True)
    pg = spread(pg.reshape((groups, groups) + pg.shape[1:]), "x").astype(BF16)
    pg = (spread(pg, "y") * (1.0 / math.sqrt(tokens))).astype(BF16)
    pg_pieces = from_others(jnp.stack(from_others(pg, "y")), "x")
    layer = project(heads, cols, attn_rows, w_pieces)
    dq, dk, dv, proj_grad = unpack(cols, grad_rows, pg_pieces)
    return layer[None], dq[None], dk[None], dv[None], proj_grad


def solution(mesh):
    split = Mesh(mesh.devices.reshape(8, 2, 4, 4), ("z", "c", "x", "y"))
    rows = P(("x", "y"), ("z", "c"), None)
    in_specs = (rows, rows, rows, rows, P(("z", "c"), None), P(("z", "c"), None, None))
    out_specs = (rows, rows, rows, rows, P(("z", "c"), None))
    return jax.shard_map(body, mesh=split, in_specs=in_specs, out_specs=out_specs, check_vma=False)
```

```python
import functools
import math

import jax
import jax.numpy as jnp
from jax import lax
from jax.experimental import pallas as pl
from jax.experimental.pallas import tpu as pltpu
from jax.sharding import Mesh
from jax.sharding import PartitionSpec as P

HEAD_DIM = 128
BLOCK = 128
INV_ROOT = 1.0 / math.sqrt(HEAD_DIM)
LOG2E = 1.0 / math.log(2.0)
BF16 = jnp.bfloat16
F32 = jnp.float32
VM = pl.BlockSpec(memory_space=pltpu.VMEM)
SM = pl.BlockSpec(memory_space=pltpu.SMEM)
HBM = pl.BlockSpec(memory_space=pltpu.HBM)
MIB = 1024 * 1024


def in_hbm(value):
    return pltpu.with_memory_space_constraint(value, pltpu.HBM)


def like(*shape, dtype=BF16):
    return jax.ShapeDtypeStruct(shape, dtype)


def pack_kernel(
    place_ref, q_ref, k_ref, v_ref, g_ref, w_ref, qkv_ref, gw_ref, held, qkv_held, gw_held, sem
):
    count = qkv_ref.shape[0]
    cut = pl.ds(pl.multiple_of(place_ref[0] * BLOCK, BLOCK), BLOCK)
    loads = [
        pltpu.make_async_copy(source, held.at[n], sem.at[n])
        for n, source in enumerate((g_ref, q_ref, k_ref, v_ref))
    ]
    loads.append(pltpu.make_async_copy(w_ref.at[:, cut], gw_held.at[count], sem.at[4]))
    for copy in loads:
        copy.start()
    loads[0].wait()
    loads[4].wait()
    for j in range(count):
        gw_held[j] = held[0, :, j * BLOCK : (j + 1) * BLOCK]
    gw_out = pltpu.make_async_copy(gw_held, gw_ref, sem.at[5])
    gw_out.start()
    for n in range(3):
        loads[n + 1].wait()
        for j in range(count):
            qkv_held[j, n] = held[n + 1, :, j * BLOCK : (j + 1) * BLOCK]
    qkv_out = pltpu.make_async_copy(qkv_held, qkv_ref, sem.at[6])
    qkv_out.start()
    gw_out.wait()
    qkv_out.wait()


def pack(place, q, k, v, g, w):
    count = q.shape[1] // BLOCK
    return pl.pallas_call(
        pack_kernel,
        out_shape=(
            pltpu.HBM((count, 3, BLOCK, BLOCK), BF16),
            pltpu.HBM((count + 1, BLOCK, BLOCK), BF16),
        ),
        in_specs=[SM] + [HBM] * 5,
        out_specs=(HBM, HBM),
        scratch_shapes=[
            pltpu.VMEM((4,) + q.shape, BF16),
            pltpu.VMEM((count, 3, BLOCK, BLOCK), BF16),
            pltpu.VMEM((count + 1, BLOCK, BLOCK), BF16),
            pltpu.SemaphoreType.DMA((7,)),
        ],
        compiler_params=pltpu.CompilerParams(vmem_limit_bytes=24 * MIB),
        name="pack",
    )(place, *(in_hbm(value) for value in (q, k, v, g, w)))


def rows_of(c):
    return pl.ds(pl.multiple_of(c * BLOCK, BLOCK), BLOCK)


def forward_kernel(blocks_ref, qkv_ref, attn_ref, attn_t_ref, lse_ref, vt_ref):
    block_count, slot_count = blocks_ref.shape

    def prepare(c, carry):
        vt_ref[c] = qkv_ref[c, 2].T
        return carry

    lax.fori_loop(0, block_count, prepare, 0, unroll=4)

    def one(b):
        owners = [blocks_ref[b, s] for s in range(slot_count)]
        keys = jnp.concatenate([qkv_ref[c, 1] for c in owners], axis=0)
        scores = jnp.dot(keys, qkv_ref[b, 0].T, preferred_element_type=F32)
        top = jnp.max(scores, axis=0, keepdims=True)
        raised = jnp.exp2((scores - top) * (INV_ROOT * LOG2E))
        total = jnp.sum(raised, axis=0, keepdims=True)
        prob = (raised * (1.0 / total)).astype(BF16)
        v_t = jnp.concatenate([vt_ref[c] for c in owners], axis=1)
        attn_t = jnp.dot(v_t, prob, preferred_element_type=F32).astype(BF16)
        attn_t_ref[b] = attn_t
        attn_ref[b] = attn_t.T
        lse_ref[b] = top * (INV_ROOT * LOG2E) + jnp.log2(total)

    def step(i, carry):
        one(2 * i)
        one(2 * i + 1)
        return carry

    lax.fori_loop(0, block_count // 2, step, 0)


def forward(blocks, qkv):
    count = qkv.shape[0]
    return pl.pallas_call(
        forward_kernel,
        out_shape=(
            like(count, BLOCK, HEAD_DIM),
            like(count, HEAD_DIM, BLOCK),
            like(count, 1, BLOCK, dtype=F32),
        ),
        in_specs=[SM, VM],
        out_specs=(VM, VM, VM),
        scratch_shapes=[pltpu.VMEM((count, HEAD_DIM, BLOCK), BF16)],
        compiler_params=pltpu.CompilerParams(vmem_limit_bytes=24 * MIB),
        name="forward",
    )(blocks, qkv)


def loads_of(parts, g_refs, g_buf, sem):
    found = {}
    for n, (pair, low, high) in enumerate(parts):
        copy = pltpu.make_async_copy(
            g_refs[n].at[pl.ds(0, high - low)], g_buf.at[pair, pl.ds(low, high - low)], sem.at[n]
        )
        copy.start()
        found.setdefault(pair, []).append(copy)
    return found


def side_by_side(g_buf, pair):
    return jnp.concatenate([g_buf[pair, j] for j in range(g_buf.shape[1])], axis=1)


def attn_grad_kernel(parts, mine_ref, theirs_ref, *refs):
    g_refs = refs[: len(parts)]
    d_mine_ref, d_theirs_ref, g_buf, wt_ref, sem = refs[len(parts) :]
    loads = loads_of(parts, g_refs, g_buf, sem)
    wt_ref[:, :HEAD_DIM] = mine_ref[...].T
    wt_ref[:, HEAD_DIM:] = theirs_ref[...].T
    for pair, copies in loads.items():
        for copy in copies:
            copy.wait()
        found = jnp.dot(
            side_by_side(g_buf, pair), wt_ref[...], preferred_element_type=F32
        ).astype(BF16)
        d_mine_ref[pair] = found[:, :HEAD_DIM]
        d_theirs_ref[pair] = found[:, HEAD_DIM:]


def shard_scratch(parts, chunks):
    pairs = 1 + max(pair for pair, _, _ in parts)
    return [pltpu.VMEM((pairs, chunks, BLOCK, BLOCK), BF16)], [pltpu.SemaphoreType.DMA((len(parts),))]


def attn_grad(parts, mine, theirs, shards):
    buf, sem = shard_scratch(parts, mine.shape[1] // BLOCK)
    pairs = buf[0].shape[0]
    return pl.pallas_call(
        functools.partial(attn_grad_kernel, parts),
        out_shape=(like(pairs, BLOCK, HEAD_DIM),) * 2,
        in_specs=[VM, VM] + [HBM] * len(shards),
        out_specs=(VM, VM),
        scratch_shapes=buf + [pltpu.VMEM((mine.shape[1], 2 * HEAD_DIM), BF16)] + sem,
        compiler_params=pltpu.CompilerParams(vmem_limit_bytes=24 * MIB),
        name="attn_grad",
    )(mine, theirs, *(in_hbm(shard) for shard in shards))


def weight_grad_kernel(parts, place_ref, attn_ref, other_ref, *refs):
    g_refs = refs[: len(parts)]
    mine_ref, theirs_ref, g_buf, acc_ref, sem = refs[len(parts) :]
    loads = loads_of(parts, g_refs, g_buf, sem)
    pairs = list(loads)
    chips = len(pairs)
    for step in range(0, chips, 2):
        two = pairs[step : step + 2]
        left = []
        for pair in two:
            for copy in loads[pair]:
                copy.wait()
            chip = lax.rem(place_ref[0] + place_ref[2 + pair], chips)
            left.append(
                jnp.concatenate([attn_ref[2 * chip + place_ref[1]], other_ref[chip]], axis=0)
            )
        found = jnp.dot(
            jnp.concatenate(left, axis=1),
            jnp.concatenate([side_by_side(g_buf, pair) for pair in two], axis=0),
            preferred_element_type=F32,
        )
        if step:
            acc_ref[...] += found
        else:
            acc_ref[...] = found
    for j in range(mine_ref.shape[0]):
        cols = slice(j * BLOCK, (j + 1) * BLOCK)
        mine_ref[j] = acc_ref[:HEAD_DIM, cols].astype(BF16)
        theirs_ref[j] = acc_ref[HEAD_DIM:, cols].astype(BF16)


def weight_grad(parts, place, attn_t, other_t, chunks, shards):
    buf, sem = shard_scratch(parts, chunks)
    return pl.pallas_call(
        functools.partial(weight_grad_kernel, parts),
        out_shape=(like(chunks, HEAD_DIM, BLOCK),) * 2,
        in_specs=[SM, VM, VM] + [HBM] * len(shards),
        out_specs=(VM, VM),
        scratch_shapes=buf + [pltpu.VMEM((2 * HEAD_DIM, chunks * BLOCK), F32)] + sem,
        compiler_params=pltpu.CompilerParams(vmem_limit_bytes=24 * MIB),
        name="weight_grad",
    )(place, attn_t, other_t, *(in_hbm(shard) for shard in shards))


def backward_kernel(
    blocks_ref, place_ref, qkv_ref, attn_t_ref, lse_ref, early_ref, theirs_early_ref, late_ref,
    theirs_late_ref, out_ref, kv_ref, kt_ref, acc_ref, mine_ref, theirs_ref,
):
    block_count, slot_count = blocks_ref.shape
    half = block_count // 2
    zero = jnp.zeros((BLOCK, HEAD_DIM), BF16)

    def prepare(c, carry):
        k_one, v_one = qkv_ref[c, 1], qkv_ref[c, 2]
        kv_ref[rows_of(c), :] = jnp.concatenate([k_one, v_one], axis=1)
        kt_ref[c] = k_one.T
        acc_ref[rows_of(c), :] = jnp.zeros((BLOCK, 2 * HEAD_DIM), F32)
        return carry

    lax.fori_loop(0, block_count, prepare, 0, unroll=2)
    first = early_ref.shape[0]
    mine_ref[:first] = early_ref[...]
    mine_ref[first:] = late_ref[...]
    theirs_ref[:first] = theirs_early_ref[...]
    theirs_ref[first:] = theirs_late_ref[...]

    def one(b, d_one):
        q_one = qkv_ref[b, 0]
        q_t, d_t = q_one.T, d_one.T
        owners = [blocks_ref[b, s] for s in range(slot_count)]
        right = jnp.concatenate(
            [jnp.concatenate([q_t, zero], axis=1), jnp.concatenate([zero, d_t], axis=1)], axis=0
        )
        kv = jnp.concatenate([kv_ref[rows_of(c), :] for c in owners], axis=0)
        both = jnp.dot(kv, right, preferred_element_type=F32)
        scores, prob_grad = both[:, :BLOCK], both[:, BLOCK:]
        prob = jnp.exp2(scores * (INV_ROOT * LOG2E) - lse_ref[b])
        row_dot = jnp.sum(attn_t_ref[b].astype(F32) * d_t.astype(F32), axis=0, keepdims=True)
        score_grad = (prob * (prob_grad - row_dot) * INV_ROOT).astype(BF16)
        k_t = jnp.concatenate([kt_ref[c] for c in owners], axis=1)
        dq_t = jnp.dot(k_t, score_grad, preferred_element_type=F32)
        out_ref[b, 0] = dq_t.astype(BF16).T
        back = jnp.concatenate(
            [jnp.concatenate([q_one, zero], axis=1), jnp.concatenate([zero, d_one], axis=1)], axis=0
        )
        return owners, jnp.dot(
            jnp.concatenate([score_grad, prob.astype(BF16)], axis=1),
            back,
            preferred_element_type=F32,
        )

    def step(i, carry):
        chip = lax.rem(place_ref[0] + place_ref[2 + i], half)
        results = [
            one(2 * chip + place_ref[1], mine_ref[i]),
            one(2 * chip + 1 - place_ref[1], theirs_ref[i]),
        ]
        for owners, found in results:
            for s, c in enumerate(owners):
                acc_ref[rows_of(c), :] += found[s * BLOCK : (s + 1) * BLOCK, :]
        return carry

    lax.fori_loop(0, half, step, 0)

    def finish(c, carry):
        out_ref[c, 1] = acc_ref[rows_of(c), :HEAD_DIM].astype(BF16)
        out_ref[c, 2] = acc_ref[rows_of(c), HEAD_DIM:].astype(BF16)
        return carry

    lax.fori_loop(0, block_count, finish, 0, unroll=2)


def backward(blocks, place, qkv, attn_t, lse, *attn_grads):
    count = qkv.shape[0]
    return pl.pallas_call(
        backward_kernel,
        out_shape=like(count, 3, BLOCK, HEAD_DIM),
        in_specs=[SM, SM] + [VM] * (3 + len(attn_grads)),
        out_specs=VM,
        scratch_shapes=[
            pltpu.VMEM((count * BLOCK, 2 * HEAD_DIM), BF16),
            pltpu.VMEM((count, HEAD_DIM, BLOCK), BF16),
            pltpu.VMEM((count * BLOCK, 2 * HEAD_DIM), F32),
            pltpu.VMEM((count // 2, BLOCK, HEAD_DIM), BF16),
            pltpu.VMEM((count // 2, BLOCK, HEAD_DIM), BF16),
        ],
        compiler_params=pltpu.CompilerParams(vmem_limit_bytes=24 * MIB),
        name="backward",
    )(blocks, place, qkv, attn_t, lse, *attn_grads)


def collect_kernel(spots, *refs):
    w_refs, out_ref, sem = refs[: len(spots)], refs[-2], refs[-1]
    copies = [
        pltpu.make_async_copy(w_ref.at[spot], out_ref.at[n], sem.at[n])
        for n, (w_ref, spot) in enumerate(zip(w_refs, spots))
    ]
    for copy in copies:
        copy.start()
    for copy in copies:
        copy.wait()


def collect(spots, arrays):
    return pl.pallas_call(
        functools.partial(collect_kernel, spots),
        out_shape=like(len(spots), BLOCK, BLOCK),
        in_specs=[HBM] * len(spots),
        out_specs=VM,
        scratch_shapes=[pltpu.SemaphoreType.DMA((len(spots),))],
        name="collect",
    )(*(in_hbm(array) for array in arrays))


def project_kernel(groups, heads_ref, cols_ref, *refs):
    row_refs, w_refs = refs[:groups], refs[groups : 3 * groups]
    part_refs, rows_buf = refs[3 * groups : 4 * groups], refs[-1]
    half = w_refs[0].shape[0]
    for i in range(groups):
        for e in range(2 * half):
            rows_buf[i * BLOCK : (i + 1) * BLOCK, e * HEAD_DIM : (e + 1) * HEAD_DIM] = row_refs[i][
                heads_ref[e]
            ]
    rows = rows_buf[...]
    for j in range(0, groups, 2):
        weights = jnp.concatenate(
            [
                jnp.concatenate(
                    [w_refs[side * groups + t][...].reshape(half * HEAD_DIM, BLOCK) for side in range(2)],
                    axis=0,
                )
                for t in (j, j + 1)
            ],
            axis=1,
        )
        found = jnp.dot(rows, weights, preferred_element_type=F32).astype(BF16)
        for n in range(2):
            at = pl.ds(pl.multiple_of(cols_ref[j + n] * BLOCK, BLOCK), BLOCK)
            for i in range(groups):
                part_refs[i][:, at] = found[
                    i * BLOCK : (i + 1) * BLOCK, n * BLOCK : (n + 1) * BLOCK
                ]


def project(heads, cols, rows, weights):
    groups = len(rows)
    width = rows[0].shape[0] * HEAD_DIM
    return pl.pallas_call(
        functools.partial(project_kernel, groups),
        out_shape=(like(BLOCK, groups * BLOCK),) * groups,
        in_specs=[SM, SM] + [VM] * (3 * groups),
        out_specs=(VM,) * groups,
        scratch_shapes=[pltpu.VMEM((groups * BLOCK, width), BF16)],
        compiler_params=pltpu.CompilerParams(vmem_limit_bytes=24 * MIB),
        name="project",
    )(heads, cols, *rows, *weights)


def unpack_kernel(groups, cols_ref, places_ref, grads_ref, *refs):
    layer_refs, pg_refs = refs[:groups], refs[groups : 2 * groups]
    layer_ref, dq_ref, dk_ref, dv_ref, pg_ref = refs[2 * groups :]
    for h in range(grads_ref.shape[0]):
        cols = slice(h * HEAD_DIM, (h + 1) * HEAD_DIM)
        dq_ref[:, cols] = grads_ref[h, 0]
        dk_ref[:, cols] = grads_ref[h, 1]
        dv_ref[:, cols] = grads_ref[h, 2]
    wide = layer_refs[0].shape[1]
    for i in range(groups):
        layer_ref[:, pl.ds(pl.multiple_of(places_ref[i] * wide, wide), wide)] = layer_refs[i][...]
        for j in range(groups):
            at = pl.multiple_of(cols_ref[i * groups + j] * BLOCK, BLOCK)
            pg_ref[:, pl.ds(at, BLOCK)] = pg_refs[i][j].astype(F32)


def unpack(cols, places, grads, layers, pg_pieces):
    wide = like(BLOCK, grads.shape[0] * HEAD_DIM)
    groups = len(pg_pieces)
    return pl.pallas_call(
        functools.partial(unpack_kernel, groups),
        out_shape=(
            like(BLOCK, groups * layers[0].shape[1]),
            wide,
            wide,
            wide,
            like(HEAD_DIM, groups * groups * BLOCK, dtype=F32),
        ),
        in_specs=[SM, SM, VM] + [VM] * (2 * groups),
        out_specs=(VM,) * 5,
        compiler_params=pltpu.CompilerParams(vmem_limit_bytes=24 * MIB),
        name="unpack",
    )(cols, places, grads, *layers, *pg_pieces)


def shifted(value, axis, by):
    size = lax.axis_size(axis)
    return lax.ppermute(value, axis, [(i, (i + by) % size) for i in range(size)])


def from_others(value, axis):
    return [value] + [shifted(value, axis, i) for i in range(1, lax.axis_size(axis))]


def spread(value, axis):
    size = lax.axis_size(axis)
    here = lax.axis_index(axis)
    total = lax.dynamic_index_in_dim(value, here, 0, keepdims=False).astype(F32)
    for i in range(1, size):
        piece = lax.dynamic_index_in_dim(value, (here + i) % size, 0, keepdims=False)
        total = total + shifted(piece, axis, i).astype(F32)
    return total


def swapped(value):
    return lax.ppermute(value, "c", [(0, 1), (1, 0)])


def body(query_in, key_in, value_in, out_grad, out_proj, key_blocks):
    seq, dp = ("z", "c"), ("x", "y")
    chips = lax.axis_size("z")
    core, z = lax.axis_index("c").astype(jnp.int32), lax.axis_index("z").astype(jnp.int32)
    x, y = lax.axis_index("x").astype(jnp.int32), lax.axis_index("y").astype(jnp.int32)
    tokens = lax.axis_size(seq) * lax.axis_size(dp) * query_in.shape[1]
    groups = lax.axis_size("x")
    chunks = out_proj.shape[1] // BLOCK
    blocks = key_blocks[0]
    index = jnp.arange(groups, dtype=jnp.int32)

    place = (x * groups + y)[None]
    qkv_out, gw = pack(place, query_in[0], key_in[0], value_in[0], out_grad[0], out_proj)
    qkv = lax.all_to_all(qkv_out, seq, split_axis=0, concat_axis=0, tiled=True)
    proj_theirs = swapped(out_proj)

    shifts, parts, shards = [0], [(0, 0, chunks)], [gw]
    up = down = gw
    for k in range(1, chips // 2):
        if k == chips // 2 - 1:
            qkv, up, down = lax.optimization_barrier((qkv, up, down))
        up, down = shifted(up, "z", 1), shifted(down, "z", -1)
        for shift, array in ((-k, up), (k, down)):
            parts.append((len(shifts), 0, chunks))
            shifts.append(shift)
            shards.append(array)
    cut = chunks // 2
    parts += [(len(shifts), 0, cut), (len(shifts), cut, chunks)]
    shifts.append(chips // 2)
    shards += [shifted(up[:cut], "z", 1), shifted(down[cut:], "z", -1)]
    parts = tuple(parts)
    steps = jnp.array([s % chips for s in shifts], jnp.int32)
    spot = jnp.concatenate([jnp.stack([z, core]), steps])

    attn, attn_t, lse = forward(blocks, qkv)
    other_t = swapped(
        lax.dynamic_index_in_dim(
            attn_t.reshape((chips, 2) + attn_t.shape[1:]), 1 - core, 1, keepdims=False
        )
    )
    early, theirs_early = attn_grad(parts[:-2], out_proj, proj_theirs, shards[:-2])
    theirs_early = swapped(theirs_early)
    attn, shards[-2], shards[-1] = lax.optimization_barrier((attn, shards[-2], shards[-1]))
    attn_rows = lax.all_to_all(attn, seq, split_axis=0, concat_axis=0, tiled=True)
    late, theirs_late = attn_grad(
        ((0, 0, cut), (0, cut, chunks)), out_proj, proj_theirs, shards[-2:]
    )
    theirs_late = swapped(theirs_late)
    spots = tuple([chunks] * (chips - 1) + [chunks - cut])
    own_weights = collect(spots, shards[: chips - 1] + shards[-1:])
    theirs_late, own_weights = lax.optimization_barrier((theirs_late, own_weights))
    weights = from_others(own_weights, "y")
    grads = backward(blocks, spot, qkv, attn_t, lse, early, theirs_early, late, theirs_late)
    grad_rows = lax.all_to_all(grads, seq, split_axis=0, concat_axis=0, tiled=True)

    weights += [swapped(piece) for piece in weights]
    rows = from_others(attn_rows, "x")
    owner = 2 * ((z + steps) % chips)
    heads = jnp.concatenate([owner + core, owner + 1 - core])
    found = project(heads, (y - index) % groups, rows, weights)
    layers = [part if i == 0 else shifted(part, "x", -i) for i, part in enumerate(found)]

    other_t, _ = lax.optimization_barrier((other_t, rows))
    pg_mine, pg_theirs = weight_grad(parts, spot, attn_t, other_t, chunks, shards)
    pg = (pg_mine.astype(F32) + swapped(pg_theirs).astype(F32)).astype(BF16)
    pg = spread(pg.reshape((groups, groups) + pg.shape[1:]), "x").astype(BF16)
    pg = (spread(pg, "y") * (1.0 / math.sqrt(tokens))).astype(BF16)
    pg_pieces = from_others(jnp.stack(from_others(pg, "y")), "x")
    cols = (((x - index) % groups)[:, None] * groups + ((y - index) % groups)[None]).reshape(-1)

    layer, dq, dk, dv, proj_grad = unpack(cols, (x + index) % groups, grad_rows, layers, pg_pieces)
    return layer[None], dq[None], dk[None], dv[None], proj_grad


def solution(mesh):
    split = Mesh(mesh.devices.reshape(8, 2, 4, 4), ("z", "c", "x", "y"))
    rows = P(("x", "y"), ("z", "c"), None)
    in_specs = (rows, rows, rows, rows, P(("z", "c"), None), P(("z", "c"), None, None))
    out_specs = (rows, rows, rows, rows, P(("z", "c"), None))
    return jax.shard_map(body, mesh=split, in_specs=in_specs, out_specs=out_specs, check_vma=False)
```

```python
import functools
import math

import jax
import jax.numpy as jnp
from jax import lax
from jax.experimental import pallas as pl
from jax.experimental.pallas import tpu as pltpu
from jax.sharding import Mesh
from jax.sharding import PartitionSpec as P

HEAD_DIM = 128
BLOCK = 128
INV_ROOT = 1.0 / math.sqrt(HEAD_DIM)
LOG2E = 1.0 / math.log(2.0)
BF16 = jnp.bfloat16
F32 = jnp.float32
VM = pl.BlockSpec(memory_space=pltpu.VMEM)
SM = pl.BlockSpec(memory_space=pltpu.SMEM)
HBM = pl.BlockSpec(memory_space=pltpu.HBM)
MIB = 1024 * 1024
QUERY = slice(0, BLOCK)
KEY = slice(BLOCK, 2 * BLOCK)
VALUE = slice(2 * BLOCK, 3 * BLOCK)
SENT = 3 * BLOCK + BLOCK // 2
MICROSECOND = 1_150_000_000


def cost(flops):
    return pl.CostEstimate(flops=flops, bytes_accessed=0, transcendentals=0)


def in_hbm(value):
    return pltpu.with_memory_space_constraint(value, pltpu.HBM)


def like(*shape, dtype=BF16):
    return jax.ShapeDtypeStruct(shape, dtype)


def pack_kernel(
    place_ref, q_ref, k_ref, v_ref, g_ref, w_ref, qkv_ref, g_out_ref, held, w_held, qkv_held,
    g_held, sem,
):
    count = qkv_ref.shape[0]
    cut = pl.ds(pl.multiple_of(place_ref[0] * BLOCK, BLOCK), BLOCK)
    half = BLOCK // 2
    loads = [
        pltpu.make_async_copy(source, held.at[n], sem.at[n])
        for n, source in enumerate((g_ref, q_ref, k_ref, v_ref))
    ]
    loads.append(pltpu.make_async_copy(w_ref.at[:, cut], w_held, sem.at[4]))
    for copy in loads:
        copy.start()
    loads[0].wait()
    for j in range(count):
        g_held[j] = held[0, :, j * BLOCK : (j + 1) * BLOCK]
    g_out = pltpu.make_async_copy(g_held, g_out_ref, sem.at[5])
    g_out.start()
    loads[4].wait()
    for j in range(count):
        qkv_held[j, 3 * BLOCK :] = w_held[(j % 2) * half : (j % 2 + 1) * half, :]
    for n in range(3):
        loads[n + 1].wait()
        for j in range(count):
            qkv_held[j, n * BLOCK : (n + 1) * BLOCK] = held[
                n + 1, :, j * BLOCK : (j + 1) * BLOCK
            ]
    qkv_out = pltpu.make_async_copy(qkv_held, qkv_ref, sem.at[6])
    qkv_out.start()
    g_out.wait()
    qkv_out.wait()


def pack(place, q, k, v, g, w):
    count = q.shape[1] // BLOCK
    return pl.pallas_call(
        pack_kernel,
        out_shape=(
            pltpu.HBM((count, SENT, BLOCK), BF16),
            pltpu.HBM((count, BLOCK, BLOCK), BF16),
        ),
        in_specs=[SM] + [HBM] * 5,
        out_specs=(HBM, HBM),
        scratch_shapes=[
            pltpu.VMEM((4,) + q.shape, BF16),
            pltpu.VMEM((BLOCK, BLOCK), BF16),
            pltpu.VMEM((count, SENT, BLOCK), BF16),
            pltpu.VMEM((count, BLOCK, BLOCK), BF16),
            pltpu.SemaphoreType.DMA((7,)),
        ],
        compiler_params=pltpu.CompilerParams(vmem_limit_bytes=24 * MIB),
        cost_estimate=cost(3 * MICROSECOND),
        name="pack",
    )(place, *(in_hbm(value) for value in (q, k, v, g, w)))


def rows_of(c):
    return pl.ds(pl.multiple_of(c * BLOCK, BLOCK), BLOCK)


def forward_kernel(blocks_ref, qkv_ref, attn_ref, attn_t_ref, lse_ref, vt_ref):
    block_count, slot_count = blocks_ref.shape

    def prepare(c, carry):
        vt_ref[c] = qkv_ref[c, VALUE].T
        return carry

    lax.fori_loop(0, block_count, prepare, 0, unroll=4)

    def one(b):
        owners = [blocks_ref[b, s] for s in range(slot_count)]
        keys = jnp.concatenate([qkv_ref[c, KEY] for c in owners], axis=0)
        scores = jnp.dot(keys, qkv_ref[b, QUERY].T, preferred_element_type=F32)
        top = jnp.max(scores, axis=0, keepdims=True)
        raised = jnp.exp2((scores - top) * (INV_ROOT * LOG2E))
        total = jnp.sum(raised, axis=0, keepdims=True)
        prob = (raised * (1.0 / total)).astype(BF16)
        v_t = jnp.concatenate([vt_ref[c] for c in owners], axis=1)
        attn_t = jnp.dot(v_t, prob, preferred_element_type=F32).astype(BF16)
        attn_t_ref[b] = attn_t
        attn_ref[b] = attn_t.T
        lse_ref[b] = top * (INV_ROOT * LOG2E) + jnp.log2(total)

    def step(i, carry):
        one(2 * i)
        one(2 * i + 1)
        return carry

    lax.fori_loop(0, block_count // 2, step, 0)


def forward(blocks, qkv):
    count = qkv.shape[0]
    return pl.pallas_call(
        forward_kernel,
        out_shape=(
            like(count, BLOCK, HEAD_DIM),
            like(count, HEAD_DIM, BLOCK),
            like(count, 1, BLOCK, dtype=F32),
        ),
        in_specs=[SM, VM],
        out_specs=(VM, VM, VM),
        scratch_shapes=[pltpu.VMEM((count, HEAD_DIM, BLOCK), BF16)],
        compiler_params=pltpu.CompilerParams(vmem_limit_bytes=24 * MIB),
        cost_estimate=cost(12 * MICROSECOND),
        name="forward",
    )(blocks, qkv)


def loads_of(parts, g_refs, g_buf, sem):
    found = {}
    for n, (pair, low, high) in enumerate(parts):
        copy = pltpu.make_async_copy(
            g_refs[n].at[pl.ds(0, high - low)], g_buf.at[pair, pl.ds(low, high - low)], sem.at[n]
        )
        copy.start()
        found.setdefault(pair, []).append(copy)
    return found


def side_by_side(g_buf, pair):
    return jnp.concatenate([g_buf[pair, j] for j in range(g_buf.shape[1])], axis=1)


def attn_grad_kernel(parts, mine_ref, theirs_ref, *refs):
    g_refs = refs[: len(parts)]
    d_mine_ref, d_theirs_ref, g_buf, wt_ref, sem = refs[len(parts) :]
    loads = loads_of(parts, g_refs, g_buf, sem)
    wt_ref[:, :HEAD_DIM] = mine_ref[...].T
    wt_ref[:, HEAD_DIM:] = theirs_ref[...].T
    for pair, copies in loads.items():
        for copy in copies:
            copy.wait()
        found = jnp.dot(
            side_by_side(g_buf, pair), wt_ref[...], preferred_element_type=F32
        ).astype(BF16)
        d_mine_ref[pair] = found[:, :HEAD_DIM]
        d_theirs_ref[pair] = found[:, HEAD_DIM:]


def shard_scratch(parts, chunks):
    pairs = 1 + max(pair for pair, _, _ in parts)
    return [pltpu.VMEM((pairs, chunks, BLOCK, BLOCK), BF16)], [pltpu.SemaphoreType.DMA((len(parts),))]


def attn_grad(parts, mine, theirs, shards):
    buf, sem = shard_scratch(parts, mine.shape[1] // BLOCK)
    pairs = buf[0].shape[0]
    return pl.pallas_call(
        functools.partial(attn_grad_kernel, parts),
        out_shape=(like(pairs, BLOCK, HEAD_DIM),) * 2,
        in_specs=[VM, VM] + [HBM] * len(shards),
        out_specs=(VM, VM),
        scratch_shapes=buf + [pltpu.VMEM((mine.shape[1], 2 * HEAD_DIM), BF16)] + sem,
        compiler_params=pltpu.CompilerParams(vmem_limit_bytes=24 * MIB),
        cost_estimate=cost(4 * MICROSECOND),
        name="attn_grad",
    )(mine, theirs, *(in_hbm(shard) for shard in shards))


def weight_grad_kernel(parts, place_ref, attn_ref, other_ref, *refs):
    g_refs = refs[: len(parts)]
    mine_ref, theirs_ref, g_buf, acc_ref, sem = refs[len(parts) :]
    loads = loads_of(parts, g_refs, g_buf, sem)
    pairs = list(loads)
    chips = len(pairs)
    for step in range(0, chips, 2):
        two = pairs[step : step + 2]
        left = []
        for pair in two:
            for copy in loads[pair]:
                copy.wait()
            chip = lax.rem(place_ref[0] + place_ref[2 + pair], chips)
            left.append(
                jnp.concatenate([attn_ref[2 * chip + place_ref[1]], other_ref[chip]], axis=0)
            )
        found = jnp.dot(
            jnp.concatenate(left, axis=1),
            jnp.concatenate([side_by_side(g_buf, pair) for pair in two], axis=0),
            preferred_element_type=F32,
        )
        if step:
            acc_ref[...] += found
        else:
            acc_ref[...] = found
    for j in range(mine_ref.shape[0]):
        cols = slice(j * BLOCK, (j + 1) * BLOCK)
        mine_ref[j] = acc_ref[:HEAD_DIM, cols].astype(BF16)
        theirs_ref[j] = acc_ref[HEAD_DIM:, cols].astype(BF16)


def weight_grad(parts, place, attn_t, other_t, chunks, shards):
    buf, sem = shard_scratch(parts, chunks)
    return pl.pallas_call(
        functools.partial(weight_grad_kernel, parts),
        out_shape=(like(chunks, HEAD_DIM, BLOCK),) * 2,
        in_specs=[SM, VM, VM] + [HBM] * len(shards),
        out_specs=(VM, VM),
        scratch_shapes=buf + [pltpu.VMEM((2 * HEAD_DIM, chunks * BLOCK), F32)] + sem,
        compiler_params=pltpu.CompilerParams(vmem_limit_bytes=24 * MIB),
        cost_estimate=cost(4 * MICROSECOND),
        name="weight_grad",
    )(place, attn_t, other_t, *(in_hbm(shard) for shard in shards))


def backward_kernel(
    blocks_ref, place_ref, qkv_ref, attn_t_ref, lse_ref, early_ref, theirs_early_ref, late_ref,
    theirs_late_ref, out_ref, kv_ref, kt_ref, acc_ref, mine_ref, theirs_ref,
):
    block_count, slot_count = blocks_ref.shape
    half = block_count // 2
    zero = jnp.zeros((BLOCK, HEAD_DIM), BF16)

    def prepare(c, carry):
        k_one, v_one = qkv_ref[c, KEY], qkv_ref[c, VALUE]
        kv_ref[rows_of(c), :] = jnp.concatenate([k_one, v_one], axis=1)
        kt_ref[c] = k_one.T
        acc_ref[rows_of(c), :] = jnp.zeros((BLOCK, 2 * HEAD_DIM), F32)
        return carry

    lax.fori_loop(0, block_count, prepare, 0, unroll=2)
    first = early_ref.shape[0]
    mine_ref[:first] = early_ref[...]
    mine_ref[first:] = late_ref[...]
    theirs_ref[:first] = theirs_early_ref[...]
    theirs_ref[first:] = theirs_late_ref[...]

    def one(b, d_one):
        q_one = qkv_ref[b, QUERY]
        q_t, d_t = q_one.T, d_one.T
        owners = [blocks_ref[b, s] for s in range(slot_count)]
        right = jnp.concatenate(
            [jnp.concatenate([q_t, zero], axis=1), jnp.concatenate([zero, d_t], axis=1)], axis=0
        )
        kv = jnp.concatenate([kv_ref[rows_of(c), :] for c in owners], axis=0)
        both = jnp.dot(kv, right, preferred_element_type=F32)
        scores, prob_grad = both[:, :BLOCK], both[:, BLOCK:]
        prob = jnp.exp2(scores * (INV_ROOT * LOG2E) - lse_ref[b])
        row_dot = jnp.sum(attn_t_ref[b].astype(F32) * d_t.astype(F32), axis=0, keepdims=True)
        score_grad = (prob * (prob_grad - row_dot) * INV_ROOT).astype(BF16)
        k_t = jnp.concatenate([kt_ref[c] for c in owners], axis=1)
        dq_t = jnp.dot(k_t, score_grad, preferred_element_type=F32)
        out_ref[b, 0] = dq_t.astype(BF16).T
        back = jnp.concatenate(
            [jnp.concatenate([q_one, zero], axis=1), jnp.concatenate([zero, d_one], axis=1)], axis=0
        )
        return owners, jnp.dot(
            jnp.concatenate([score_grad, prob.astype(BF16)], axis=1),
            back,
            preferred_element_type=F32,
        )

    def step(i, carry):
        chip = lax.rem(place_ref[0] + place_ref[2 + i], half)
        results = [
            one(2 * chip + place_ref[1], mine_ref[i]),
            one(2 * chip + 1 - place_ref[1], theirs_ref[i]),
        ]
        for owners, found in results:
            for s, c in enumerate(owners):
                acc_ref[rows_of(c), :] += found[s * BLOCK : (s + 1) * BLOCK, :]
        return carry

    lax.fori_loop(0, half, step, 0)

    def finish(c, carry):
        out_ref[c, 1] = acc_ref[rows_of(c), :HEAD_DIM].astype(BF16)
        out_ref[c, 2] = acc_ref[rows_of(c), HEAD_DIM:].astype(BF16)
        return carry

    lax.fori_loop(0, block_count, finish, 0, unroll=2)


def backward(blocks, place, qkv, attn_t, lse, *attn_grads):
    count = qkv.shape[0]
    return pl.pallas_call(
        backward_kernel,
        out_shape=like(count, 3, BLOCK, HEAD_DIM),
        in_specs=[SM, SM] + [VM] * (3 + len(attn_grads)),
        out_specs=VM,
        scratch_shapes=[
            pltpu.VMEM((count * BLOCK, 2 * HEAD_DIM), BF16),
            pltpu.VMEM((count, HEAD_DIM, BLOCK), BF16),
            pltpu.VMEM((count * BLOCK, 2 * HEAD_DIM), F32),
            pltpu.VMEM((count // 2, BLOCK, HEAD_DIM), BF16),
            pltpu.VMEM((count // 2, BLOCK, HEAD_DIM), BF16),
        ],
        compiler_params=pltpu.CompilerParams(vmem_limit_bytes=24 * MIB),
        cost_estimate=cost(13 * MICROSECOND),
        name="backward",
    )(blocks, place, qkv, attn_t, lse, *attn_grads)


def project_kernel(pieces, cols_ref, core_ref, mine_ref, *refs):
    own_refs, other_refs = refs[: len(pieces)], refs[len(pieces) : 2 * len(pieces)]
    layer_ref, rows_buf = refs[2 * len(pieces) :]
    count = mine_ref.shape[0]
    for h in range(count):
        rows_buf[:, h * HEAD_DIM : (h + 1) * HEAD_DIM] = mine_ref[h]
    rows = rows_buf[...]
    lower = core_ref[0] == 0
    groups = max(high for _, _, high in pieces)
    for n, (shift, low, high) in enumerate(pieces):
        for j in range(0, high - low, 2):
            weights = []
            for t in (j, j + 1):
                own, other = own_refs[n][t], other_refs[n][t]
                first = jnp.where(lower, own, other)
                second = jnp.where(lower, other, own)
                weights.append(
                    jnp.concatenate([first, second], axis=1).reshape(count * HEAD_DIM, BLOCK)
                )
            found = jnp.dot(
                rows, jnp.concatenate(weights, axis=1), preferred_element_type=F32
            ).astype(BF16)
            for t in range(2):
                at = pl.multiple_of(cols_ref[shift * groups + low + j + t] * BLOCK, BLOCK)
                layer_ref[:, pl.ds(at, BLOCK)] = found[:, t * BLOCK : (t + 1) * BLOCK]


def project(pieces, cols, core, mine, own, other):
    count = mine.shape[0]
    return pl.pallas_call(
        functools.partial(project_kernel, pieces),
        out_shape=like(BLOCK, cols.shape[0] * BLOCK),
        in_specs=[SM, SM] + [VM] * (1 + 2 * len(pieces)),
        out_specs=VM,
        scratch_shapes=[pltpu.VMEM((BLOCK, count * HEAD_DIM), BF16)],
        compiler_params=pltpu.CompilerParams(vmem_limit_bytes=32 * MIB),
        cost_estimate=cost(6 * MICROSECOND),
        name="project",
    )(cols, core, mine, *own, *other)


def unpack_kernel(groups, places_ref, grads_ref, *refs):
    part_refs = refs[:groups]
    dq_ref, dk_ref, dv_ref, pg_ref = refs[groups:]
    for h in range(grads_ref.shape[0]):
        cols = slice(h * HEAD_DIM, (h + 1) * HEAD_DIM)
        dq_ref[:, cols] = grads_ref[h, 0]
        dk_ref[:, cols] = grads_ref[h, 1]
        dv_ref[:, cols] = grads_ref[h, 2]
    wide = groups * BLOCK
    for i in range(groups):
        for t in range(groups):
            at = pl.ds(pl.multiple_of(places_ref[i] * wide + t * BLOCK, BLOCK), BLOCK)
            pg_ref[:, at] = part_refs[i][t].astype(F32)


def unpack(places, grads, parts):
    wide = like(BLOCK, grads.shape[0] * HEAD_DIM)
    groups = len(parts)
    return pl.pallas_call(
        functools.partial(unpack_kernel, groups),
        out_shape=(wide, wide, wide, like(HEAD_DIM, groups * groups * BLOCK, dtype=F32)),
        in_specs=[SM, VM] + [VM] * groups,
        out_specs=(VM,) * 4,
        compiler_params=pltpu.CompilerParams(vmem_limit_bytes=24 * MIB),
        cost_estimate=cost(3 * MICROSECOND),
        name="unpack",
    )(places, grads, *parts)


def shifted(value, axis, by):
    size = lax.axis_size(axis)
    return lax.ppermute(value, axis, [(i, (i + by) % size) for i in range(size)])


def from_others(value, axis):
    return [value] + [shifted(value, axis, i) for i in range(1, lax.axis_size(axis))]


def spread(value, axis):
    size = lax.axis_size(axis)
    here = lax.axis_index(axis)
    total = lax.dynamic_index_in_dim(value, here, 0, keepdims=False).astype(F32)
    for i in range(1, size):
        piece = lax.dynamic_index_in_dim(value, (here + i) % size, 0, keepdims=False)
        total = total + shifted(piece, axis, i).astype(F32)
    return total


def swapped(value):
    return lax.ppermute(value, "c", [(0, 1), (1, 0)])


def body(query_in, key_in, value_in, out_grad, out_proj, key_blocks):
    seq, dp = ("z", "c"), ("x", "y")
    chips = lax.axis_size("z")
    core, z = lax.axis_index("c").astype(jnp.int32), lax.axis_index("z").astype(jnp.int32)
    x, y = lax.axis_index("x").astype(jnp.int32), lax.axis_index("y").astype(jnp.int32)
    tokens = lax.axis_size(seq) * lax.axis_size(dp) * query_in.shape[1]
    groups = lax.axis_size("x")
    chunks = out_proj.shape[1] // BLOCK
    blocks = key_blocks[0]
    index = jnp.arange(groups, dtype=jnp.int32)

    place = (x * groups + y)[None]
    qkv_out, gw = pack(place, query_in[0], key_in[0], value_in[0], out_grad[0], out_proj)
    qkv = lax.all_to_all(qkv_out, seq, split_axis=0, concat_axis=0, tiled=True)
    proj_theirs = swapped(out_proj)

    shifts, parts, shards = [0], [(0, 0, chunks)], [gw]
    up = down = gw
    for k in range(1, chips // 2):
        if k == 2:
            qkv, up, down = lax.optimization_barrier((qkv, up, down))
            w_near = from_others(qkv[:, 3 * BLOCK :], "y")
        if k == 3:
            up, down, w_near = lax.optimization_barrier((up, down, w_near))
            w_here = jnp.stack(w_near)
            w_up, w_down = shifted(w_here, "x", 1), shifted(w_here, "x", -1)
        up, down = shifted(up, "z", 1), shifted(down, "z", -1)
        for shift, array in ((-k, up), (k, down)):
            parts.append((len(shifts), 0, chunks))
            shifts.append(shift)
            shards.append(array)
    cut = chunks // 2
    attn, attn_t, lse = forward(blocks, qkv)
    attn, up, down = lax.optimization_barrier((attn, up, down))
    shards += [shifted(up[:cut], "z", 1), shifted(down[cut:], "z", -1)]
    parts += [(len(shifts), 0, cut), (len(shifts), cut, chunks)]
    shifts.append(chips // 2)
    parts = tuple(parts)
    steps = jnp.array([s % chips for s in shifts], jnp.int32)
    spot = jnp.concatenate([jnp.stack([z, core]), steps])

    other_t = swapped(
        lax.dynamic_index_in_dim(
            attn_t.reshape((chips, 2) + attn_t.shape[1:]), 1 - core, 1, keepdims=False
        )
    )
    early, theirs_early = attn_grad(parts[:-2], out_proj, proj_theirs, shards[:-2])
    theirs_early = swapped(theirs_early)
    attn, early, shards[-2], shards[-1], w_up, w_down = lax.optimization_barrier(
        (attn, early, shards[-2], shards[-1], w_up, w_down)
    )
    attn_rows = lax.all_to_all(attn, seq, split_axis=0, concat_axis=0, tiled=True)
    late, theirs_late = attn_grad(
        ((0, 0, cut), (0, cut, chunks)), out_proj, proj_theirs, shards[-2:]
    )
    theirs_late = swapped(theirs_late)
    middle = groups // 2
    w_far = [shifted(w_up[:middle], "x", 1), shifted(w_down[middle:], "x", -1)]
    grads = backward(blocks, spot, qkv, attn_t, lse, early, theirs_early, late, theirs_late)
    grads, attn_rows, w_far, other_t = lax.optimization_barrier((grads, attn_rows, w_far, other_t))
    grad_rows = lax.all_to_all(grads, seq, split_axis=0, concat_axis=0, tiled=True)

    pg_mine, pg_theirs = weight_grad(parts, spot, attn_t, other_t, chunks, shards)
    pg = (pg_mine.astype(F32) + swapped(pg_theirs).astype(F32)).astype(BF16)
    pg = spread(pg.reshape((groups, groups) + pg.shape[1:]), "x").astype(BF16)
    pieces = ((0, 0, groups), (1, 0, groups), (groups - 1, 0, groups))
    pieces += ((middle, 0, middle), (middle, middle, groups))
    weights = [w_here, w_up, w_down] + w_far
    cols = (((x - index) % groups)[:, None] * groups + ((y - index) % groups)[None]).reshape(-1)
    layer = project(pieces, cols, core[None], attn_rows, weights, [swapped(w) for w in weights])
    pg, layer = lax.optimization_barrier((pg, layer))
    pg = sum(piece.astype(F32) for piece in from_others(pg, "y"))
    pg = (pg * (1.0 / math.sqrt(tokens))).astype(BF16)
    pg_pieces = from_others(pg, "x")
    dq, dk, dv, proj_grad = unpack((x - index) % groups, grad_rows, pg_pieces)
    return layer[None], dq[None], dk[None], dv[None], proj_grad


def solution(mesh):
    split = Mesh(mesh.devices.reshape(8, 2, 4, 4), ("z", "c", "x", "y"))
    rows = P(("x", "y"), ("z", "c"), None)
    in_specs = (rows, rows, rows, rows, P(("z", "c"), None), P(("z", "c"), None, None))
    out_specs = (rows, rows, rows, rows, P(("z", "c"), None))
    return jax.shard_map(body, mesh=split, in_specs=in_specs, out_specs=out_specs, check_vma=False)
```

```python
import functools
import math

import jax
import jax.numpy as jnp
from jax import lax
from jax.experimental import pallas as pl
from jax.experimental.pallas import tpu as pltpu
from jax.sharding import Mesh
from jax.sharding import PartitionSpec as P

HEAD_DIM = 128
BLOCK = 128
INV_ROOT = 1.0 / math.sqrt(HEAD_DIM)
LOG2E = 1.0 / math.log(2.0)
BF16 = jnp.bfloat16
F32 = jnp.float32
VM = pl.BlockSpec(memory_space=pltpu.VMEM)
SM = pl.BlockSpec(memory_space=pltpu.SMEM)
HBM = pl.BlockSpec(memory_space=pltpu.HBM)
MIB = 1024 * 1024
QUERY = slice(0, BLOCK)
KEY = slice(BLOCK, 2 * BLOCK)
VALUE = slice(2 * BLOCK, 3 * BLOCK)
SENT = 3 * BLOCK + BLOCK // 2
MICROSECOND = 1_150_000_000


def cost(flops):
    return pl.CostEstimate(flops=flops, bytes_accessed=0, transcendentals=0)


def in_hbm(value):
    return pltpu.with_memory_space_constraint(value, pltpu.HBM)


def like(*shape, dtype=BF16):
    return jax.ShapeDtypeStruct(shape, dtype)


def pack_kernel(
    place_ref, q_ref, k_ref, v_ref, g_ref, w_ref, qkv_ref, g_out_ref, held, w_held, qkv_held,
    g_held, sem,
):
    count = qkv_ref.shape[0]
    cut = pl.ds(pl.multiple_of(place_ref[0] * BLOCK, BLOCK), BLOCK)
    half = BLOCK // 2
    loads = [
        pltpu.make_async_copy(source, held.at[n], sem.at[n])
        for n, source in enumerate((g_ref, q_ref, k_ref, v_ref))
    ]
    loads.append(pltpu.make_async_copy(w_ref.at[:, cut], w_held, sem.at[4]))
    for copy in loads:
        copy.start()
    loads[0].wait()
    for j in range(count):
        g_held[j] = held[0, :, j * BLOCK : (j + 1) * BLOCK]
    g_out = pltpu.make_async_copy(g_held, g_out_ref, sem.at[5])
    g_out.start()
    loads[4].wait()
    for j in range(count):
        qkv_held[j, 3 * BLOCK :] = w_held[(j % 2) * half : (j % 2 + 1) * half, :]
    for n in range(3):
        loads[n + 1].wait()
        for j in range(count):
            qkv_held[j, n * BLOCK : (n + 1) * BLOCK] = held[
                n + 1, :, j * BLOCK : (j + 1) * BLOCK
            ]
    qkv_out = pltpu.make_async_copy(qkv_held, qkv_ref, sem.at[6])
    qkv_out.start()
    g_out.wait()
    qkv_out.wait()


def pack(place, q, k, v, g, w):
    count = q.shape[1] // BLOCK
    return pl.pallas_call(
        pack_kernel,
        out_shape=(
            pltpu.HBM((count, SENT, BLOCK), BF16),
            pltpu.HBM((count, BLOCK, BLOCK), BF16),
        ),
        in_specs=[SM] + [HBM] * 5,
        out_specs=(HBM, HBM),
        scratch_shapes=[
            pltpu.VMEM((4,) + q.shape, BF16),
            pltpu.VMEM((BLOCK, BLOCK), BF16),
            pltpu.VMEM((count, SENT, BLOCK), BF16),
            pltpu.VMEM((count, BLOCK, BLOCK), BF16),
            pltpu.SemaphoreType.DMA((7,)),
        ],
        compiler_params=pltpu.CompilerParams(vmem_limit_bytes=24 * MIB),
        cost_estimate=cost(3 * MICROSECOND),
        name="pack",
    )(place, *(in_hbm(value) for value in (q, k, v, g, w)))


def rows_of(c):
    return pl.ds(pl.multiple_of(c * BLOCK, BLOCK), BLOCK)


def forward_kernel(blocks_ref, qkv_ref, attn_ref, attn_t_ref, lse_ref, vt_ref):
    block_count, slot_count = blocks_ref.shape

    def prepare(c, carry):
        vt_ref[c] = qkv_ref[c, VALUE].T
        return carry

    lax.fori_loop(0, block_count, prepare, 0, unroll=4)

    def one(b):
        owners = [blocks_ref[b, s] for s in range(slot_count)]
        keys = jnp.concatenate([qkv_ref[c, KEY] for c in owners], axis=0)
        scores = jnp.dot(keys, qkv_ref[b, QUERY].T, preferred_element_type=F32)
        top = jnp.max(scores, axis=0, keepdims=True)
        raised = jnp.exp2((scores - top) * (INV_ROOT * LOG2E))
        total = jnp.sum(raised, axis=0, keepdims=True)
        prob = (raised * (1.0 / total)).astype(BF16)
        v_t = jnp.concatenate([vt_ref[c] for c in owners], axis=1)
        attn_t = jnp.dot(v_t, prob, preferred_element_type=F32).astype(BF16)
        attn_t_ref[b] = attn_t
        attn_ref[b] = attn_t.T
        lse_ref[b] = top * (INV_ROOT * LOG2E) + jnp.log2(total)

    def step(i, carry):
        one(2 * i)
        one(2 * i + 1)
        return carry

    lax.fori_loop(0, block_count // 2, step, 0)


def forward(blocks, qkv):
    count = qkv.shape[0]
    return pl.pallas_call(
        forward_kernel,
        out_shape=(
            like(count, BLOCK, HEAD_DIM),
            like(count, HEAD_DIM, BLOCK),
            like(count, 1, BLOCK, dtype=F32),
        ),
        in_specs=[SM, VM],
        out_specs=(VM, VM, VM),
        scratch_shapes=[pltpu.VMEM((count, HEAD_DIM, BLOCK), BF16)],
        compiler_params=pltpu.CompilerParams(vmem_limit_bytes=24 * MIB),
        cost_estimate=cost(12 * MICROSECOND),
        name="forward",
    )(blocks, qkv)


def loads_of(parts, g_refs, g_buf, sem):
    found = {}
    for n, (pair, low, high) in enumerate(parts):
        copy = pltpu.make_async_copy(
            g_refs[n].at[pl.ds(0, high - low)], g_buf.at[pair, pl.ds(low, high - low)], sem.at[n]
        )
        copy.start()
        found.setdefault(pair, []).append(copy)
    return found


def side_by_side(g_buf, pair):
    return jnp.concatenate([g_buf[pair, j] for j in range(g_buf.shape[1])], axis=1)


def attn_grad_kernel(parts, mine_ref, theirs_ref, *refs):
    g_refs = refs[: len(parts)]
    d_mine_ref, d_theirs_ref, g_buf, wt_ref, sem = refs[len(parts) :]
    loads = loads_of(parts, g_refs, g_buf, sem)
    wt_ref[:, :HEAD_DIM] = mine_ref[...].T
    wt_ref[:, HEAD_DIM:] = theirs_ref[...].T
    for pair, copies in loads.items():
        for copy in copies:
            copy.wait()
        found = jnp.dot(
            side_by_side(g_buf, pair), wt_ref[...], preferred_element_type=F32
        ).astype(BF16)
        d_mine_ref[pair] = found[:, :HEAD_DIM]
        d_theirs_ref[pair] = found[:, HEAD_DIM:]


def shard_scratch(parts, chunks):
    pairs = 1 + max(pair for pair, _, _ in parts)
    return [pltpu.VMEM((pairs, chunks, BLOCK, BLOCK), BF16)], [pltpu.SemaphoreType.DMA((len(parts),))]


def attn_grad(parts, mine, theirs, shards):
    buf, sem = shard_scratch(parts, mine.shape[1] // BLOCK)
    pairs = buf[0].shape[0]
    return pl.pallas_call(
        functools.partial(attn_grad_kernel, parts),
        out_shape=(like(pairs, BLOCK, HEAD_DIM),) * 2,
        in_specs=[VM, VM] + [HBM] * len(shards),
        out_specs=(VM, VM),
        scratch_shapes=buf + [pltpu.VMEM((mine.shape[1], 2 * HEAD_DIM), BF16)] + sem,
        compiler_params=pltpu.CompilerParams(vmem_limit_bytes=24 * MIB),
        cost_estimate=cost(4 * MICROSECOND),
        name="attn_grad",
    )(mine, theirs, *(in_hbm(shard) for shard in shards))


def weight_grad_kernel(parts, place_ref, attn_ref, other_ref, *refs):
    g_refs = refs[: len(parts)]
    mine_ref, theirs_ref, g_buf, acc_ref, sem = refs[len(parts) :]
    loads = loads_of(parts, g_refs, g_buf, sem)
    pairs = list(loads)
    chips = len(pairs)
    for step in range(0, chips, 2):
        two = pairs[step : step + 2]
        left = []
        for pair in two:
            for copy in loads[pair]:
                copy.wait()
            chip = lax.rem(place_ref[0] + place_ref[2 + pair], chips)
            left.append(
                jnp.concatenate([attn_ref[2 * chip + place_ref[1]], other_ref[chip]], axis=0)
            )
        found = jnp.dot(
            jnp.concatenate(left, axis=1),
            jnp.concatenate([side_by_side(g_buf, pair) for pair in two], axis=0),
            preferred_element_type=F32,
        )
        if step:
            acc_ref[...] += found
        else:
            acc_ref[...] = found
    for j in range(mine_ref.shape[0]):
        cols = slice(j * BLOCK, (j + 1) * BLOCK)
        mine_ref[j] = acc_ref[:HEAD_DIM, cols].astype(BF16)
        theirs_ref[j] = acc_ref[HEAD_DIM:, cols].astype(BF16)


def weight_grad(parts, place, attn_t, other_t, chunks, shards):
    buf, sem = shard_scratch(parts, chunks)
    return pl.pallas_call(
        functools.partial(weight_grad_kernel, parts),
        out_shape=(like(chunks, HEAD_DIM, BLOCK),) * 2,
        in_specs=[SM, VM, VM] + [HBM] * len(shards),
        out_specs=(VM, VM),
        scratch_shapes=buf + [pltpu.VMEM((2 * HEAD_DIM, chunks * BLOCK), F32)] + sem,
        compiler_params=pltpu.CompilerParams(vmem_limit_bytes=24 * MIB),
        cost_estimate=cost(4 * MICROSECOND),
        name="weight_grad",
    )(place, attn_t, other_t, *(in_hbm(shard) for shard in shards))


def backward_kernel(
    blocks_ref, place_ref, qkv_ref, attn_t_ref, lse_ref, early_ref, theirs_early_ref, late_ref,
    theirs_late_ref, out_ref, kv_ref, kt_ref, acc_ref, mine_ref, theirs_ref,
):
    block_count, slot_count = blocks_ref.shape
    half = block_count // 2
    zero = jnp.zeros((BLOCK, HEAD_DIM), BF16)

    def prepare(c, carry):
        k_one, v_one = qkv_ref[c, KEY], qkv_ref[c, VALUE]
        kv_ref[rows_of(c), :] = jnp.concatenate([k_one, v_one], axis=1)
        kt_ref[c] = k_one.T
        acc_ref[rows_of(c), :] = jnp.zeros((BLOCK, 2 * HEAD_DIM), F32)
        return carry

    lax.fori_loop(0, block_count, prepare, 0, unroll=2)
    first = early_ref.shape[0]
    mine_ref[:first] = early_ref[...]
    mine_ref[first:] = late_ref[...]
    theirs_ref[:first] = theirs_early_ref[...]
    theirs_ref[first:] = theirs_late_ref[...]

    def one(b, d_one):
        q_one = qkv_ref[b, QUERY]
        q_t, d_t = q_one.T, d_one.T
        owners = [blocks_ref[b, s] for s in range(slot_count)]
        right = jnp.concatenate(
            [jnp.concatenate([q_t, zero], axis=1), jnp.concatenate([zero, d_t], axis=1)], axis=0
        )
        lse = lse_ref[b]
        row_dot = jnp.sum(attn_t_ref[b].astype(F32) * d_t.astype(F32), axis=0, keepdims=True)
        pairs = []
        for c in owners:
            both = jnp.dot(kv_ref[rows_of(c), :], right, preferred_element_type=F32)
            prob = jnp.exp2(both[:, :BLOCK] * (INV_ROOT * LOG2E) - lse)
            score_grad = (prob * (both[:, BLOCK:] - row_dot) * INV_ROOT).astype(BF16)
            pairs.append((score_grad, prob.astype(BF16)))
        back = jnp.concatenate(
            [jnp.concatenate([q_one, zero], axis=1), jnp.concatenate([zero, d_one], axis=1)], axis=0
        )
        for c, pair in zip(owners, pairs):
            acc_ref[rows_of(c), :] += jnp.dot(
                jnp.concatenate(pair, axis=1), back, preferred_element_type=F32
            )
        k_t = jnp.concatenate([kt_ref[c] for c in owners], axis=1)
        score_grads = jnp.concatenate([score_grad for score_grad, _ in pairs], axis=0)
        dq_t = jnp.dot(k_t, score_grads, preferred_element_type=F32)
        out_ref[b, 0] = dq_t.astype(BF16).T

    def step(i, carry):
        chip = lax.rem(place_ref[0] + place_ref[2 + i], half)
        one(2 * chip + place_ref[1], mine_ref[i])
        one(2 * chip + 1 - place_ref[1], theirs_ref[i])
        return carry

    lax.fori_loop(0, half, step, 0)

    def finish(c, carry):
        out_ref[c, 1] = acc_ref[rows_of(c), :HEAD_DIM].astype(BF16)
        out_ref[c, 2] = acc_ref[rows_of(c), HEAD_DIM:].astype(BF16)
        return carry

    lax.fori_loop(0, block_count, finish, 0, unroll=2)


def backward(blocks, place, qkv, attn_t, lse, *attn_grads):
    count = qkv.shape[0]
    return pl.pallas_call(
        backward_kernel,
        out_shape=like(count, 3, BLOCK, HEAD_DIM),
        in_specs=[SM, SM] + [VM] * (3 + len(attn_grads)),
        out_specs=VM,
        scratch_shapes=[
            pltpu.VMEM((count * BLOCK, 2 * HEAD_DIM), BF16),
            pltpu.VMEM((count, HEAD_DIM, BLOCK), BF16),
            pltpu.VMEM((count * BLOCK, 2 * HEAD_DIM), F32),
            pltpu.VMEM((count // 2, BLOCK, HEAD_DIM), BF16),
            pltpu.VMEM((count // 2, BLOCK, HEAD_DIM), BF16),
        ],
        compiler_params=pltpu.CompilerParams(vmem_limit_bytes=24 * MIB),
        cost_estimate=cost(13 * MICROSECOND),
        name="backward",
    )(blocks, place, qkv, attn_t, lse, *attn_grads)


def project_kernel(pieces, cols_ref, core_ref, mine_ref, *refs):
    own_refs, other_refs = refs[: len(pieces)], refs[len(pieces) : 2 * len(pieces)]
    layer_ref, rows_buf = refs[2 * len(pieces) :]
    count = mine_ref.shape[0]
    for h in range(count):
        rows_buf[:, h * HEAD_DIM : (h + 1) * HEAD_DIM] = mine_ref[h]
    rows = rows_buf[...]
    lower = core_ref[0] == 0
    groups = max(high for _, _, high in pieces)
    for n, (shift, low, high) in enumerate(pieces):
        for j in range(0, high - low, 2):
            weights = []
            for t in (j, j + 1):
                own, other = own_refs[n][t], other_refs[n][t]
                first = jnp.where(lower, own, other)
                second = jnp.where(lower, other, own)
                weights.append(
                    jnp.concatenate([first, second], axis=1).reshape(count * HEAD_DIM, BLOCK)
                )
            found = jnp.dot(
                rows, jnp.concatenate(weights, axis=1), preferred_element_type=F32
            ).astype(BF16)
            for t in range(2):
                at = pl.multiple_of(cols_ref[shift * groups + low + j + t] * BLOCK, BLOCK)
                layer_ref[:, pl.ds(at, BLOCK)] = found[:, t * BLOCK : (t + 1) * BLOCK]


def project(pieces, cols, core, mine, own, other):
    count = mine.shape[0]
    return pl.pallas_call(
        functools.partial(project_kernel, pieces),
        out_shape=like(BLOCK, cols.shape[0] * BLOCK),
        in_specs=[SM, SM] + [VM] * (1 + 2 * len(pieces)),
        out_specs=VM,
        scratch_shapes=[pltpu.VMEM((BLOCK, count * HEAD_DIM), BF16)],
        compiler_params=pltpu.CompilerParams(vmem_limit_bytes=32 * MIB),
        cost_estimate=cost(6 * MICROSECOND),
        name="project",
    )(cols, core, mine, *(in_hbm(w) for w in own + other))


def unpack_kernel(groups, places_ref, grads_ref, *refs):
    part_refs = refs[:groups]
    dq_ref, dk_ref, dv_ref, pg_ref = refs[groups:]
    for h in range(grads_ref.shape[0]):
        cols = slice(h * HEAD_DIM, (h + 1) * HEAD_DIM)
        dq_ref[:, cols] = grads_ref[h, 0]
        dk_ref[:, cols] = grads_ref[h, 1]
        dv_ref[:, cols] = grads_ref[h, 2]
    wide = groups * BLOCK
    for i in range(groups):
        for t in range(groups):
            at = pl.ds(pl.multiple_of(places_ref[i] * wide + t * BLOCK, BLOCK), BLOCK)
            pg_ref[:, at] = part_refs[i][t].astype(F32)


def unpack(places, grads, parts):
    wide = like(BLOCK, grads.shape[0] * HEAD_DIM)
    groups = len(parts)
    return pl.pallas_call(
        functools.partial(unpack_kernel, groups),
        out_shape=(wide, wide, wide, like(HEAD_DIM, groups * groups * BLOCK, dtype=F32)),
        in_specs=[SM, VM] + [VM] * groups,
        out_specs=(VM,) * 4,
        compiler_params=pltpu.CompilerParams(vmem_limit_bytes=24 * MIB),
        cost_estimate=cost(3 * MICROSECOND),
        name="unpack",
    )(places, grads, *parts)


def shifted(value, axis, by):
    size = lax.axis_size(axis)
    return lax.ppermute(value, axis, [(i, (i + by) % size) for i in range(size)])


def from_others(value, axis):
    return [value] + [shifted(value, axis, i) for i in range(1, lax.axis_size(axis))]


def exchanged(value, axis):
    size = lax.axis_size(axis)
    here = lax.axis_index(axis)
    pieces = [
        lax.dynamic_index_in_dim(value, (here + i) % size, 0, keepdims=False) for i in range(size)
    ]
    return pieces[:1] + [shifted(piece, axis, i) for i, piece in enumerate(pieces) if i]


def total_of(pieces):
    return sum(piece.astype(F32) for piece in pieces)


def swapped(value):
    return lax.ppermute(value, "c", [(0, 1), (1, 0)])


def body(query_in, key_in, value_in, out_grad, out_proj, key_blocks):
    seq, dp = ("z", "c"), ("x", "y")
    chips = lax.axis_size("z")
    core, z = lax.axis_index("c").astype(jnp.int32), lax.axis_index("z").astype(jnp.int32)
    x, y = lax.axis_index("x").astype(jnp.int32), lax.axis_index("y").astype(jnp.int32)
    tokens = lax.axis_size(seq) * lax.axis_size(dp) * query_in.shape[1]
    groups = lax.axis_size("x")
    chunks = out_proj.shape[1] // BLOCK
    blocks = key_blocks[0]
    index = jnp.arange(groups, dtype=jnp.int32)

    place = (x * groups + y)[None]
    qkv_out, gw = pack(place, query_in[0], key_in[0], value_in[0], out_grad[0], out_proj)
    qkv = lax.all_to_all(qkv_out, seq, split_axis=0, concat_axis=0, tiled=True)
    proj_theirs = swapped(out_proj)

    shifts, parts, shards = [0], [(0, 0, chunks)], [gw]
    up = down = gw
    for k in range(1, chips // 2):
        if k == 2:
            qkv, up, down = lax.optimization_barrier((qkv, up, down))
            w_near = from_others(qkv[:, 3 * BLOCK :], "y")
        if k == 3:
            up, down, w_near = lax.optimization_barrier((up, down, w_near))
            w_here = jnp.stack(w_near)
            w_up, w_down = shifted(w_here, "x", 1), shifted(w_here, "x", -1)
        up, down = shifted(up, "z", 1), shifted(down, "z", -1)
        for shift, array in ((-k, up), (k, down)):
            parts.append((len(shifts), 0, chunks))
            shifts.append(shift)
            shards.append(array)
    cut = chunks // 2
    attn, attn_t, lse = forward(blocks, qkv)
    attn, up, down = lax.optimization_barrier((attn, up, down))
    shards += [shifted(up[:cut], "z", 1), shifted(down[cut:], "z", -1)]
    parts += [(len(shifts), 0, cut), (len(shifts), cut, chunks)]
    shifts.append(chips // 2)
    parts = tuple(parts)
    steps = jnp.array([s % chips for s in shifts], jnp.int32)
    spot = jnp.concatenate([jnp.stack([z, core]), steps])

    other_t = swapped(
        lax.dynamic_index_in_dim(
            attn_t.reshape((chips, 2) + attn_t.shape[1:]), 1 - core, 1, keepdims=False
        )
    )
    early, theirs_early = attn_grad(parts[:-2], out_proj, proj_theirs, shards[:-2])
    theirs_early = swapped(theirs_early)
    attn, early, shards[-2], shards[-1], w_up, w_down = lax.optimization_barrier(
        (attn, early, shards[-2], shards[-1], w_up, w_down)
    )
    attn_rows = lax.all_to_all(attn, seq, split_axis=0, concat_axis=0, tiled=True)
    late, theirs_late = attn_grad(
        ((0, 0, cut), (0, cut, chunks)), out_proj, proj_theirs, shards[-2:]
    )
    theirs_late = swapped(theirs_late)
    middle = groups // 2
    w_far = [shifted(w_up[:middle], "x", 1), shifted(w_down[middle:], "x", -1)]
    grads = backward(blocks, spot, qkv, attn_t, lse, early, theirs_early, late, theirs_late)
    grads, attn_rows, w_far, other_t = lax.optimization_barrier((grads, attn_rows, w_far, other_t))
    grad_rows = lax.all_to_all(grads, seq, split_axis=0, concat_axis=0, tiled=True)

    pg_mine, pg_theirs = weight_grad(parts, spot, attn_t, other_t, chunks, shards)
    pg = (pg_mine.astype(F32) + swapped(pg_theirs).astype(F32)).astype(BF16)
    pg_pieces = exchanged(pg.reshape((groups, groups) + pg.shape[1:]), "x")
    pieces = ((0, 0, groups), (1, 0, groups), (groups - 1, 0, groups))
    pieces += ((middle, 0, middle), (middle, middle, groups))
    weights = [w_here, w_up, w_down] + w_far
    cols = (((x - index) % groups)[:, None] * groups + ((y - index) % groups)[None]).reshape(-1)
    layer = project(pieces, cols, core[None], attn_rows, weights, [swapped(w) for w in weights])
    pg_pieces, layer = lax.optimization_barrier((pg_pieces, layer))
    pg = total_of(from_others(total_of(pg_pieces).astype(BF16), "y"))
    pg = (pg * (1.0 / math.sqrt(tokens))).astype(BF16)
    pg_pieces = from_others(pg, "x")
    dq, dk, dv, proj_grad = unpack((x - index) % groups, grad_rows, pg_pieces)
    return layer[None], dq[None], dk[None], dv[None], proj_grad


def solution(mesh):
    split = Mesh(mesh.devices.reshape(8, 2, 4, 4), ("z", "c", "x", "y"))
    rows = P(("x", "y"), ("z", "c"), None)
    in_specs = (rows, rows, rows, rows, P(("z", "c"), None), P(("z", "c"), None, None))
    out_specs = (rows, rows, rows, rows, P(("z", "c"), None))
    return jax.shard_map(body, mesh=split, in_specs=in_specs, out_specs=out_specs, check_vma=False)
```

```python
import functools
import math

import jax
import jax.numpy as jnp
from jax import lax
from jax.experimental import pallas as pl
from jax.experimental.pallas import tpu as pltpu
from jax.sharding import Mesh
from jax.sharding import PartitionSpec as P

HEAD_DIM = 128
BLOCK = 128
INV_ROOT = 1.0 / math.sqrt(HEAD_DIM)
LOG2E = 1.0 / math.log(2.0)
BF16 = jnp.bfloat16
F32 = jnp.float32
VM = pl.BlockSpec(memory_space=pltpu.VMEM)
SM = pl.BlockSpec(memory_space=pltpu.SMEM)
HBM = pl.BlockSpec(memory_space=pltpu.HBM)
MIB = 1024 * 1024
QUERY = slice(0, BLOCK)
KEY = slice(BLOCK, 2 * BLOCK)
VALUE = slice(2 * BLOCK, 3 * BLOCK)
SENT = 3 * BLOCK + BLOCK // 2
MICROSECOND = 1_150_000_000


def cost(flops):
    return pl.CostEstimate(flops=flops, bytes_accessed=0, transcendentals=0)


def in_hbm(value):
    return pltpu.with_memory_space_constraint(value, pltpu.HBM)


def like(*shape, dtype=BF16):
    return jax.ShapeDtypeStruct(shape, dtype)


def pack_kernel(
    place_ref, q_ref, k_ref, v_ref, g_ref, w_ref, qkv_ref, g_out_ref, held, w_held, qkv_held,
    g_held, sem,
):
    count = qkv_ref.shape[0]
    cut = pl.ds(pl.multiple_of(place_ref[0] * BLOCK, BLOCK), BLOCK)
    half = BLOCK // 2
    loads = [
        pltpu.make_async_copy(source, held.at[n], sem.at[n])
        for n, source in enumerate((g_ref, q_ref, k_ref, v_ref))
    ]
    loads.append(pltpu.make_async_copy(w_ref.at[:, cut], w_held, sem.at[4]))
    for copy in loads:
        copy.start()
    loads[0].wait()
    for j in range(count):
        g_held[j] = held[0, :, j * BLOCK : (j + 1) * BLOCK]
    g_out = pltpu.make_async_copy(g_held, g_out_ref, sem.at[5])
    g_out.start()
    loads[4].wait()
    for j in range(count):
        qkv_held[j, 3 * BLOCK :] = w_held[(j % 2) * half : (j % 2 + 1) * half, :]
    for n in range(3):
        loads[n + 1].wait()
        for j in range(count):
            qkv_held[j, n * BLOCK : (n + 1) * BLOCK] = held[
                n + 1, :, j * BLOCK : (j + 1) * BLOCK
            ]
    qkv_out = pltpu.make_async_copy(qkv_held, qkv_ref, sem.at[6])
    qkv_out.start()
    g_out.wait()
    qkv_out.wait()


def pack(place, q, k, v, g, w):
    count = q.shape[1] // BLOCK
    return pl.pallas_call(
        pack_kernel,
        out_shape=(
            pltpu.HBM((count, SENT, BLOCK), BF16),
            pltpu.HBM((count, BLOCK, BLOCK), BF16),
        ),
        in_specs=[SM] + [HBM] * 5,
        out_specs=(HBM, HBM),
        scratch_shapes=[
            pltpu.VMEM((4,) + q.shape, BF16),
            pltpu.VMEM((BLOCK, BLOCK), BF16),
            pltpu.VMEM((count, SENT, BLOCK), BF16),
            pltpu.VMEM((count, BLOCK, BLOCK), BF16),
            pltpu.SemaphoreType.DMA((7,)),
        ],
        compiler_params=pltpu.CompilerParams(vmem_limit_bytes=24 * MIB),
        cost_estimate=cost(3 * MICROSECOND),
        name="pack",
    )(place, *(in_hbm(value) for value in (q, k, v, g, w)))


def rows_of(c):
    return pl.ds(pl.multiple_of(c * BLOCK, BLOCK), BLOCK)


def forward_kernel(blocks_ref, qkv_ref, attn_ref, attn_t_ref, lse_ref, vt_ref):
    block_count, slot_count = blocks_ref.shape

    def prepare(c, carry):
        vt_ref[c] = qkv_ref[c, VALUE].T
        return carry

    lax.fori_loop(0, block_count, prepare, 0, unroll=4)

    def one(b):
        owners = [blocks_ref[b, s] for s in range(slot_count)]
        q_t = qkv_ref[b, QUERY].T
        scores = [jnp.dot(qkv_ref[c, KEY], q_t, preferred_element_type=F32) for c in owners]
        top = jnp.max(functools.reduce(jnp.maximum, scores), axis=0, keepdims=True)
        raised = [jnp.exp2((score - top) * (INV_ROOT * LOG2E)) for score in scores]
        total = jnp.sum(functools.reduce(jnp.add, raised), axis=0, keepdims=True)
        weights = jnp.concatenate([one_raised.astype(BF16) for one_raised in raised], axis=0)
        v_t = jnp.concatenate([vt_ref[c] for c in owners], axis=1)
        summed = jnp.dot(v_t, weights, preferred_element_type=F32)
        attn_t = (summed * (1.0 / total)).astype(BF16)
        attn_t_ref[b] = attn_t
        attn_ref[b] = attn_t.T
        lse_ref[b] = top * (INV_ROOT * LOG2E) + jnp.log2(total)

    def step(i, carry):
        one(2 * i)
        one(2 * i + 1)
        return carry

    lax.fori_loop(0, block_count // 2, step, 0)


def forward(blocks, qkv):
    count = qkv.shape[0]
    return pl.pallas_call(
        forward_kernel,
        out_shape=(
            like(count, BLOCK, HEAD_DIM),
            like(count, HEAD_DIM, BLOCK),
            like(count, 1, BLOCK, dtype=F32),
        ),
        in_specs=[SM, VM],
        out_specs=(VM, VM, VM),
        scratch_shapes=[pltpu.VMEM((count, HEAD_DIM, BLOCK), BF16)],
        compiler_params=pltpu.CompilerParams(vmem_limit_bytes=24 * MIB),
        cost_estimate=cost(12 * MICROSECOND),
        name="forward",
    )(blocks, qkv)


def loads_of(parts, g_refs, g_buf, sem):
    found = {}
    for n, (pair, low, high) in enumerate(parts):
        copy = pltpu.make_async_copy(
            g_refs[n].at[pl.ds(0, high - low)], g_buf.at[pair, pl.ds(low, high - low)], sem.at[n]
        )
        copy.start()
        found.setdefault(pair, []).append(copy)
    return found


def side_by_side(g_buf, pair):
    return jnp.concatenate([g_buf[pair, j] for j in range(g_buf.shape[1])], axis=1)


def attn_grad_kernel(parts, mine_ref, theirs_ref, *refs):
    g_refs = refs[: len(parts)]
    d_mine_ref, d_theirs_ref, g_buf, wt_ref, sem = refs[len(parts) :]
    loads = loads_of(parts, g_refs, g_buf, sem)
    wt_ref[:, :HEAD_DIM] = mine_ref[...].T
    wt_ref[:, HEAD_DIM:] = theirs_ref[...].T
    for pair, copies in loads.items():
        for copy in copies:
            copy.wait()
        found = jnp.dot(
            side_by_side(g_buf, pair), wt_ref[...], preferred_element_type=F32
        ).astype(BF16)
        d_mine_ref[pair] = found[:, :HEAD_DIM]
        d_theirs_ref[pair] = found[:, HEAD_DIM:]


def shard_scratch(parts, chunks):
    pairs = 1 + max(pair for pair, _, _ in parts)
    return [pltpu.VMEM((pairs, chunks, BLOCK, BLOCK), BF16)], [pltpu.SemaphoreType.DMA((len(parts),))]


def attn_grad(parts, mine, theirs, shards):
    buf, sem = shard_scratch(parts, mine.shape[1] // BLOCK)
    pairs = buf[0].shape[0]
    return pl.pallas_call(
        functools.partial(attn_grad_kernel, parts),
        out_shape=(like(pairs, BLOCK, HEAD_DIM),) * 2,
        in_specs=[VM, VM] + [HBM] * len(shards),
        out_specs=(VM, VM),
        scratch_shapes=buf + [pltpu.VMEM((mine.shape[1], 2 * HEAD_DIM), BF16)] + sem,
        compiler_params=pltpu.CompilerParams(vmem_limit_bytes=24 * MIB),
        cost_estimate=cost(4 * MICROSECOND),
        name="attn_grad",
    )(mine, theirs, *(in_hbm(shard) for shard in shards))


def weight_grad_kernel(parts, place_ref, attn_ref, other_ref, *refs):
    g_refs = refs[: len(parts)]
    mine_ref, theirs_ref, g_buf, acc_ref, sem = refs[len(parts) :]
    loads = loads_of(parts, g_refs, g_buf, sem)
    pairs = list(loads)
    chips = len(pairs)
    for step in range(0, chips, 2):
        two = pairs[step : step + 2]
        left = []
        for pair in two:
            for copy in loads[pair]:
                copy.wait()
            chip = lax.rem(place_ref[0] + place_ref[2 + pair], chips)
            left.append(
                jnp.concatenate([attn_ref[2 * chip + place_ref[1]], other_ref[chip]], axis=0)
            )
        found = jnp.dot(
            jnp.concatenate(left, axis=1),
            jnp.concatenate([side_by_side(g_buf, pair) for pair in two], axis=0),
            preferred_element_type=F32,
        )
        if step:
            acc_ref[...] += found
        else:
            acc_ref[...] = found
    for j in range(mine_ref.shape[0]):
        cols = slice(j * BLOCK, (j + 1) * BLOCK)
        mine_ref[j] = acc_ref[:HEAD_DIM, cols].astype(BF16)
        theirs_ref[j] = acc_ref[HEAD_DIM:, cols].astype(BF16)


def weight_grad(parts, place, attn_t, other_t, chunks, shards):
    buf, sem = shard_scratch(parts, chunks)
    return pl.pallas_call(
        functools.partial(weight_grad_kernel, parts),
        out_shape=(like(chunks, HEAD_DIM, BLOCK),) * 2,
        in_specs=[SM, VM, VM] + [HBM] * len(shards),
        out_specs=(VM, VM),
        scratch_shapes=buf + [pltpu.VMEM((2 * HEAD_DIM, chunks * BLOCK), F32)] + sem,
        compiler_params=pltpu.CompilerParams(vmem_limit_bytes=24 * MIB),
        cost_estimate=cost(4 * MICROSECOND),
        name="weight_grad",
    )(place, attn_t, other_t, *(in_hbm(shard) for shard in shards))


def backward_kernel(
    blocks_ref, place_ref, qkv_ref, attn_t_ref, lse_ref, early_ref, theirs_early_ref, late_ref,
    theirs_late_ref, out_ref, kv_ref, kt_ref, acc_ref, mine_ref, theirs_ref,
):
    block_count, slot_count = blocks_ref.shape
    half = block_count // 2
    zero = jnp.zeros((BLOCK, HEAD_DIM), BF16)

    def prepare(c, carry):
        k_one, v_one = qkv_ref[c, KEY], qkv_ref[c, VALUE]
        kv_ref[rows_of(c), :] = jnp.concatenate([k_one, v_one], axis=1)
        kt_ref[c] = k_one.T
        acc_ref[rows_of(c), :] = jnp.zeros((BLOCK, 2 * HEAD_DIM), F32)
        return carry

    lax.fori_loop(0, block_count, prepare, 0, unroll=2)
    first = early_ref.shape[0]
    mine_ref[:first] = early_ref[...]
    mine_ref[first:] = late_ref[...]
    theirs_ref[:first] = theirs_early_ref[...]
    theirs_ref[first:] = theirs_late_ref[...]

    def one(b, d_one):
        q_one = qkv_ref[b, QUERY]
        q_t, d_t = q_one.T, d_one.T
        owners = [blocks_ref[b, s] for s in range(slot_count)]
        right = jnp.concatenate(
            [jnp.concatenate([q_t, zero], axis=1), jnp.concatenate([zero, d_t], axis=1)], axis=0
        )
        lse = lse_ref[b]
        row_dot = jnp.sum(attn_t_ref[b].astype(F32) * d_t.astype(F32), axis=0, keepdims=True)
        pairs = []
        for c in owners:
            both = jnp.dot(kv_ref[rows_of(c), :], right, preferred_element_type=F32)
            prob = jnp.exp2(both[:, :BLOCK] * (INV_ROOT * LOG2E) - lse)
            score_grad = (prob * (both[:, BLOCK:] - row_dot) * INV_ROOT).astype(BF16)
            pairs.append((score_grad, prob.astype(BF16)))
        back = jnp.concatenate(
            [jnp.concatenate([q_one, zero], axis=1), jnp.concatenate([zero, d_one], axis=1)], axis=0
        )
        for c, pair in zip(owners, pairs):
            acc_ref[rows_of(c), :] += jnp.dot(
                jnp.concatenate(pair, axis=1), back, preferred_element_type=F32
            )
        k_t = jnp.concatenate([kt_ref[c] for c in owners], axis=1)
        score_grads = jnp.concatenate([score_grad for score_grad, _ in pairs], axis=0)
        dq_t = jnp.dot(k_t, score_grads, preferred_element_type=F32)
        out_ref[b, 0] = dq_t.astype(BF16).T

    def step(i, carry):
        chip = lax.rem(place_ref[0] + place_ref[2 + i], half)
        one(2 * chip + place_ref[1], mine_ref[i])
        one(2 * chip + 1 - place_ref[1], theirs_ref[i])
        return carry

    lax.fori_loop(0, half, step, 0)

    def finish(c, carry):
        out_ref[c, 1] = acc_ref[rows_of(c), :HEAD_DIM].astype(BF16)
        out_ref[c, 2] = acc_ref[rows_of(c), HEAD_DIM:].astype(BF16)
        return carry

    lax.fori_loop(0, block_count, finish, 0, unroll=2)


def backward(blocks, place, qkv, attn_t, lse, *attn_grads):
    count = qkv.shape[0]
    return pl.pallas_call(
        backward_kernel,
        out_shape=like(count, 3, BLOCK, HEAD_DIM),
        in_specs=[SM, SM] + [VM] * (3 + len(attn_grads)),
        out_specs=VM,
        scratch_shapes=[
            pltpu.VMEM((count * BLOCK, 2 * HEAD_DIM), BF16),
            pltpu.VMEM((count, HEAD_DIM, BLOCK), BF16),
            pltpu.VMEM((count * BLOCK, 2 * HEAD_DIM), F32),
            pltpu.VMEM((count // 2, BLOCK, HEAD_DIM), BF16),
            pltpu.VMEM((count // 2, BLOCK, HEAD_DIM), BF16),
        ],
        compiler_params=pltpu.CompilerParams(vmem_limit_bytes=24 * MIB),
        cost_estimate=cost(13 * MICROSECOND),
        name="backward",
    )(blocks, place, qkv, attn_t, lse, *attn_grads)


def project_kernel(pieces, cols_ref, core_ref, mine_ref, *refs):
    own_refs, other_refs = refs[: len(pieces)], refs[len(pieces) : 2 * len(pieces)]
    layer_ref, rows_buf = refs[2 * len(pieces) :]
    count = mine_ref.shape[0]
    for h in range(count):
        rows_buf[:, h * HEAD_DIM : (h + 1) * HEAD_DIM] = mine_ref[h]
    rows = rows_buf[...]
    lower = core_ref[0] == 0
    groups = max(high for _, _, high in pieces)
    for n, (shift, low, high) in enumerate(pieces):
        for j in range(0, high - low, 2):
            weights = []
            for t in (j, j + 1):
                own, other = own_refs[n][t], other_refs[n][t]
                first = jnp.where(lower, own, other)
                second = jnp.where(lower, other, own)
                weights.append(
                    jnp.concatenate([first, second], axis=1).reshape(count * HEAD_DIM, BLOCK)
                )
            found = jnp.dot(
                rows, jnp.concatenate(weights, axis=1), preferred_element_type=F32
            ).astype(BF16)
            for t in range(2):
                at = pl.multiple_of(cols_ref[shift * groups + low + j + t] * BLOCK, BLOCK)
                layer_ref[:, pl.ds(at, BLOCK)] = found[:, t * BLOCK : (t + 1) * BLOCK]


def project(pieces, cols, core, mine, own, other):
    count = mine.shape[0]
    return pl.pallas_call(
        functools.partial(project_kernel, pieces),
        out_shape=like(BLOCK, cols.shape[0] * BLOCK),
        in_specs=[SM, SM] + [VM] * (1 + 2 * len(pieces)),
        out_specs=VM,
        scratch_shapes=[pltpu.VMEM((BLOCK, count * HEAD_DIM), BF16)],
        compiler_params=pltpu.CompilerParams(vmem_limit_bytes=32 * MIB),
        cost_estimate=cost(6 * MICROSECOND),
        name="project",
    )(cols, core, mine, *(in_hbm(w) for w in own + other))


def unpack_kernel(groups, places_ref, grads_ref, *refs):
    part_refs = refs[:groups]
    dq_ref, dk_ref, dv_ref, pg_ref = refs[groups:]
    for h in range(grads_ref.shape[0]):
        cols = slice(h * HEAD_DIM, (h + 1) * HEAD_DIM)
        dq_ref[:, cols] = grads_ref[h, 0]
        dk_ref[:, cols] = grads_ref[h, 1]
        dv_ref[:, cols] = grads_ref[h, 2]
    wide = groups * BLOCK
    for i in range(groups):
        for t in range(groups):
            at = pl.ds(pl.multiple_of(places_ref[i] * wide + t * BLOCK, BLOCK), BLOCK)
            pg_ref[:, at] = part_refs[i][t].astype(F32)


def unpack(places, grads, parts):
    wide = like(BLOCK, grads.shape[0] * HEAD_DIM)
    groups = len(parts)
    return pl.pallas_call(
        functools.partial(unpack_kernel, groups),
        out_shape=(wide, wide, wide, like(HEAD_DIM, groups * groups * BLOCK, dtype=F32)),
        in_specs=[SM, VM] + [VM] * groups,
        out_specs=(VM,) * 4,
        compiler_params=pltpu.CompilerParams(vmem_limit_bytes=24 * MIB),
        cost_estimate=cost(3 * MICROSECOND),
        name="unpack",
    )(places, grads, *parts)


def shifted(value, axis, by):
    size = lax.axis_size(axis)
    return lax.ppermute(value, axis, [(i, (i + by) % size) for i in range(size)])


def from_others(value, axis):
    return [value] + [shifted(value, axis, i) for i in range(1, lax.axis_size(axis))]


def exchanged(value, axis):
    size = lax.axis_size(axis)
    here = lax.axis_index(axis)
    pieces = [
        lax.dynamic_index_in_dim(value, (here + i) % size, 0, keepdims=False) for i in range(size)
    ]
    return pieces[:1] + [shifted(piece, axis, i) for i, piece in enumerate(pieces) if i]


def total_of(pieces):
    return sum(piece.astype(F32) for piece in pieces)


def swapped(value):
    return lax.ppermute(value, "c", [(0, 1), (1, 0)])


def body(query_in, key_in, value_in, out_grad, out_proj, key_blocks):
    seq, dp = ("z", "c"), ("x", "y")
    chips = lax.axis_size("z")
    core, z = lax.axis_index("c").astype(jnp.int32), lax.axis_index("z").astype(jnp.int32)
    x, y = lax.axis_index("x").astype(jnp.int32), lax.axis_index("y").astype(jnp.int32)
    tokens = lax.axis_size(seq) * lax.axis_size(dp) * query_in.shape[1]
    groups = lax.axis_size("x")
    chunks = out_proj.shape[1] // BLOCK
    blocks = key_blocks[0]
    index = jnp.arange(groups, dtype=jnp.int32)

    place = (x * groups + y)[None]
    qkv_out, gw = pack(place, query_in[0], key_in[0], value_in[0], out_grad[0], out_proj)
    qkv = lax.all_to_all(qkv_out, seq, split_axis=0, concat_axis=0, tiled=True)
    proj_theirs = swapped(out_proj)

    shifts, parts, shards = [0], [(0, 0, chunks)], [gw]
    up = down = gw
    for k in range(1, chips // 2):
        if k == 2:
            qkv, up, down = lax.optimization_barrier((qkv, up, down))
            w_near = from_others(qkv[:, 3 * BLOCK :], "y")
        if k == 3:
            up, down, w_near = lax.optimization_barrier((up, down, w_near))
            w_here = jnp.stack(w_near)
            w_up, w_down = shifted(w_here, "x", 1), shifted(w_here, "x", -1)
        up, down = shifted(up, "z", 1), shifted(down, "z", -1)
        for shift, array in ((-k, up), (k, down)):
            parts.append((len(shifts), 0, chunks))
            shifts.append(shift)
            shards.append(array)
    cut = chunks // 2
    attn, attn_t, lse = forward(blocks, qkv)
    attn, up, down = lax.optimization_barrier((attn, up, down))
    shards += [shifted(up[:cut], "z", 1), shifted(down[cut:], "z", -1)]
    parts += [(len(shifts), 0, cut), (len(shifts), cut, chunks)]
    shifts.append(chips // 2)
    parts = tuple(parts)
    steps = jnp.array([s % chips for s in shifts], jnp.int32)
    spot = jnp.concatenate([jnp.stack([z, core]), steps])

    other_t = swapped(
        lax.dynamic_index_in_dim(
            attn_t.reshape((chips, 2) + attn_t.shape[1:]), 1 - core, 1, keepdims=False
        )
    )
    early, theirs_early = attn_grad(parts[:-2], out_proj, proj_theirs, shards[:-2])
    theirs_early = swapped(theirs_early)
    attn, early, shards[-2], shards[-1], w_up, w_down = lax.optimization_barrier(
        (attn, early, shards[-2], shards[-1], w_up, w_down)
    )
    attn_rows = lax.all_to_all(attn, seq, split_axis=0, concat_axis=0, tiled=True)
    late, theirs_late = attn_grad(
        ((0, 0, cut), (0, cut, chunks)), out_proj, proj_theirs, shards[-2:]
    )
    theirs_late = swapped(theirs_late)
    w_far = shifted(w_up, "x", 1)
    grads = backward(blocks, spot, qkv, attn_t, lse, early, theirs_early, late, theirs_late)
    grads, attn_rows, other_t = lax.optimization_barrier((grads, attn_rows, other_t))
    grad_rows = lax.all_to_all(grads, seq, split_axis=0, concat_axis=0, tiled=True)

    pg_mine, pg_theirs = weight_grad(parts, spot, attn_t, other_t, chunks, shards)
    pg_theirs, w_far = lax.optimization_barrier((pg_theirs, w_far))
    pg = (pg_mine.astype(F32) + swapped(pg_theirs).astype(F32)).astype(BF16)
    pg_pieces = exchanged(pg.reshape((groups, groups) + pg.shape[1:]), "x")
    pieces = tuple((i, 0, groups) for i in (0, 1, groups - 1, 2))
    weights = [w_here, w_up, w_down, w_far]
    cols = (((x - index) % groups)[:, None] * groups + ((y - index) % groups)[None]).reshape(-1)
    layer = project(pieces, cols, core[None], attn_rows, weights, [swapped(w) for w in weights])
    pg_pieces, layer = lax.optimization_barrier((pg_pieces, layer))
    pg = total_of(from_others(total_of(pg_pieces).astype(BF16), "y"))
    pg = (pg * (1.0 / math.sqrt(tokens))).astype(BF16)
    pg_pieces = from_others(pg, "x")
    dq, dk, dv, proj_grad = unpack((x - index) % groups, grad_rows, pg_pieces)
    return layer[None], dq[None], dk[None], dv[None], proj_grad


def solution(mesh):
    split = Mesh(mesh.devices.reshape(8, 2, 4, 4), ("z", "c", "x", "y"))
    rows = P(("x", "y"), ("z", "c"), None)
    in_specs = (rows, rows, rows, rows, P(("z", "c"), None), P(("z", "c"), None, None))
    out_specs = (rows, rows, rows, rows, P(("z", "c"), None))
    return jax.shard_map(body, mesh=split, in_specs=in_specs, out_specs=out_specs, check_vma=False)
```

```python
import functools
import math

import jax
import jax.numpy as jnp
from jax import lax
from jax.experimental import pallas as pl
from jax.experimental.pallas import tpu as pltpu
from jax.sharding import Mesh
from jax.sharding import PartitionSpec as P

HEAD_DIM = 128
BLOCK = 128
INV_ROOT = 1.0 / math.sqrt(HEAD_DIM)
LOG2E = 1.0 / math.log(2.0)
BF16 = jnp.bfloat16
F32 = jnp.float32
VM = pl.BlockSpec(memory_space=pltpu.VMEM)
SM = pl.BlockSpec(memory_space=pltpu.SMEM)
HBM = pl.BlockSpec(memory_space=pltpu.HBM)
MIB = 1024 * 1024
QUERY = slice(0, BLOCK)
KEY = slice(BLOCK, 2 * BLOCK)
VALUE = slice(2 * BLOCK, 3 * BLOCK)
SENT = 3 * BLOCK + BLOCK // 2
MICROSECOND = 1_150_000_000


def cost(flops):
    return pl.CostEstimate(flops=flops, bytes_accessed=0, transcendentals=0)


def in_hbm(value):
    return pltpu.with_memory_space_constraint(value, pltpu.HBM)


def like(*shape, dtype=BF16):
    return jax.ShapeDtypeStruct(shape, dtype)


def pack_kernel(
    place_ref, q_ref, k_ref, v_ref, g_ref, w_ref, qkv_ref, g_out_ref, held, w_held, qkv_held,
    g_held, sem,
):
    count = qkv_ref.shape[0]
    cut = pl.ds(pl.multiple_of(place_ref[0] * BLOCK, BLOCK), BLOCK)
    half = BLOCK // 2
    loads = [
        pltpu.make_async_copy(source, held.at[n], sem.at[n])
        for n, source in enumerate((g_ref, q_ref, k_ref, v_ref))
    ]
    loads.append(pltpu.make_async_copy(w_ref.at[:, cut], w_held, sem.at[4]))
    for copy in loads:
        copy.start()
    loads[0].wait()
    for j in range(count):
        g_held[j] = held[0, :, j * BLOCK : (j + 1) * BLOCK]
    g_out = pltpu.make_async_copy(g_held, g_out_ref, sem.at[5])
    g_out.start()
    loads[4].wait()
    for j in range(count):
        qkv_held[j, 3 * BLOCK :] = w_held[(j % 2) * half : (j % 2 + 1) * half, :]
    for n in range(3):
        loads[n + 1].wait()
        for j in range(count):
            qkv_held[j, n * BLOCK : (n + 1) * BLOCK] = held[
                n + 1, :, j * BLOCK : (j + 1) * BLOCK
            ]
    qkv_out = pltpu.make_async_copy(qkv_held, qkv_ref, sem.at[6])
    qkv_out.start()
    g_out.wait()
    qkv_out.wait()


def pack(place, q, k, v, g, w):
    count = q.shape[1] // BLOCK
    return pl.pallas_call(
        pack_kernel,
        out_shape=(
            pltpu.HBM((count, SENT, BLOCK), BF16),
            pltpu.HBM((count, BLOCK, BLOCK), BF16),
        ),
        in_specs=[SM] + [HBM] * 5,
        out_specs=(HBM, HBM),
        scratch_shapes=[
            pltpu.VMEM((4,) + q.shape, BF16),
            pltpu.VMEM((BLOCK, BLOCK), BF16),
            pltpu.VMEM((count, SENT, BLOCK), BF16),
            pltpu.VMEM((count, BLOCK, BLOCK), BF16),
            pltpu.SemaphoreType.DMA((7,)),
        ],
        compiler_params=pltpu.CompilerParams(vmem_limit_bytes=24 * MIB),
        cost_estimate=cost(3 * MICROSECOND),
        name="pack",
    )(place, *(in_hbm(value) for value in (q, k, v, g, w)))


def rows_of(c):
    return pl.ds(pl.multiple_of(c * BLOCK, BLOCK), BLOCK)


def forward_kernel(blocks_ref, qkv_ref, attn_ref, attn_t_ref, lse_ref, vt_ref):
    block_count, slot_count = blocks_ref.shape

    def prepare(c, carry):
        vt_ref[c] = qkv_ref[c, VALUE].T
        return carry

    lax.fori_loop(0, block_count, prepare, 0, unroll=4)

    def one(b):
        owners = [blocks_ref[b, s] for s in range(slot_count)]
        q_t = qkv_ref[b, QUERY].T
        scores = [jnp.dot(qkv_ref[c, KEY], q_t, preferred_element_type=F32) for c in owners]
        top = jnp.max(functools.reduce(jnp.maximum, scores), axis=0, keepdims=True)
        raised = [jnp.exp2((score - top) * (INV_ROOT * LOG2E)) for score in scores]
        total = jnp.sum(functools.reduce(jnp.add, raised), axis=0, keepdims=True)
        weights = jnp.concatenate([one_raised.astype(BF16) for one_raised in raised], axis=0)
        v_t = jnp.concatenate([vt_ref[c] for c in owners], axis=1)
        summed = jnp.dot(v_t, weights, preferred_element_type=F32)
        attn_t = (summed * (1.0 / total)).astype(BF16)
        attn_t_ref[b] = attn_t
        attn_ref[b] = attn_t.T
        lse_ref[b] = top * (INV_ROOT * LOG2E) + jnp.log2(total)

    def step(i, carry):
        one(2 * i)
        one(2 * i + 1)
        return carry

    lax.fori_loop(0, block_count // 2, step, 0)


def forward(blocks, qkv):
    count = qkv.shape[0]
    return pl.pallas_call(
        forward_kernel,
        out_shape=(
            like(count, BLOCK, HEAD_DIM),
            like(count, HEAD_DIM, BLOCK),
            like(count, 1, BLOCK, dtype=F32),
        ),
        in_specs=[SM, VM],
        out_specs=(VM, VM, VM),
        scratch_shapes=[pltpu.VMEM((count, HEAD_DIM, BLOCK), BF16)],
        compiler_params=pltpu.CompilerParams(vmem_limit_bytes=24 * MIB),
        cost_estimate=cost(12 * MICROSECOND),
        name="forward",
    )(blocks, qkv)


def loads_of(parts, g_refs, g_buf, sem):
    found = {}
    for n, (pair, low, high) in enumerate(parts):
        copy = pltpu.make_async_copy(
            g_refs[n].at[pl.ds(0, high - low)], g_buf.at[pair, pl.ds(low, high - low)], sem.at[n]
        )
        copy.start()
        found.setdefault(pair, []).append(copy)
    return found


def side_by_side(g_buf, pair):
    return jnp.concatenate([g_buf[pair, j] for j in range(g_buf.shape[1])], axis=1)


def attn_grad_kernel(parts, mine_ref, theirs_ref, *refs):
    g_refs = refs[: len(parts)]
    d_mine_ref, d_theirs_ref, g_buf, wt_ref, sem = refs[len(parts) :]
    loads = loads_of(parts, g_refs, g_buf, sem)
    wt_ref[:, :HEAD_DIM] = mine_ref[...].T
    wt_ref[:, HEAD_DIM:] = theirs_ref[...].T
    for pair, copies in loads.items():
        for copy in copies:
            copy.wait()
        found = jnp.dot(
            side_by_side(g_buf, pair), wt_ref[...], preferred_element_type=F32
        ).astype(BF16)
        d_mine_ref[pair] = found[:, :HEAD_DIM]
        d_theirs_ref[pair] = found[:, HEAD_DIM:]


def shard_scratch(parts, chunks):
    pairs = 1 + max(pair for pair, _, _ in parts)
    return [pltpu.VMEM((pairs, chunks, BLOCK, BLOCK), BF16)], [pltpu.SemaphoreType.DMA((len(parts),))]


def attn_grad(parts, mine, theirs, shards):
    buf, sem = shard_scratch(parts, mine.shape[1] // BLOCK)
    pairs = buf[0].shape[0]
    return pl.pallas_call(
        functools.partial(attn_grad_kernel, parts),
        out_shape=(like(pairs, BLOCK, HEAD_DIM),) * 2,
        in_specs=[VM, VM] + [HBM] * len(shards),
        out_specs=(VM, VM),
        scratch_shapes=buf + [pltpu.VMEM((mine.shape[1], 2 * HEAD_DIM), BF16)] + sem,
        compiler_params=pltpu.CompilerParams(vmem_limit_bytes=24 * MIB),
        cost_estimate=cost(4 * MICROSECOND),
        name="attn_grad",
    )(mine, theirs, *(in_hbm(shard) for shard in shards))


def weight_grad_kernel(parts, place_ref, attn_ref, other_ref, *refs):
    g_refs = refs[: len(parts)]
    mine_ref, theirs_ref, g_buf, acc_ref, sem = refs[len(parts) :]
    loads = loads_of(parts, g_refs, g_buf, sem)
    pairs = list(loads)
    chips = len(pairs)
    for step in range(0, chips, 2):
        two = pairs[step : step + 2]
        left = []
        for pair in two:
            for copy in loads[pair]:
                copy.wait()
            chip = lax.rem(place_ref[0] + place_ref[2 + pair], chips)
            left.append(
                jnp.concatenate([attn_ref[2 * chip + place_ref[1]], other_ref[chip]], axis=0)
            )
        found = jnp.dot(
            jnp.concatenate(left, axis=1),
            jnp.concatenate([side_by_side(g_buf, pair) for pair in two], axis=0),
            preferred_element_type=F32,
        )
        if step:
            acc_ref[...] += found
        else:
            acc_ref[...] = found
    for j in range(mine_ref.shape[0]):
        cols = slice(j * BLOCK, (j + 1) * BLOCK)
        mine_ref[j] = acc_ref[:HEAD_DIM, cols].astype(BF16)
        theirs_ref[j] = acc_ref[HEAD_DIM:, cols].astype(BF16)


def weight_grad(parts, place, attn_t, other_t, chunks, shards):
    buf, sem = shard_scratch(parts, chunks)
    return pl.pallas_call(
        functools.partial(weight_grad_kernel, parts),
        out_shape=(like(chunks, HEAD_DIM, BLOCK),) * 2,
        in_specs=[SM, VM, VM] + [HBM] * len(shards),
        out_specs=(VM, VM),
        scratch_shapes=buf + [pltpu.VMEM((2 * HEAD_DIM, chunks * BLOCK), F32)] + sem,
        compiler_params=pltpu.CompilerParams(vmem_limit_bytes=24 * MIB),
        cost_estimate=cost(4 * MICROSECOND),
        name="weight_grad",
    )(place, attn_t, other_t, *(in_hbm(shard) for shard in shards))


def backward_kernel(
    blocks_ref, place_ref, qkv_ref, attn_t_ref, lse_ref, early_ref, theirs_early_ref, late_ref,
    theirs_late_ref, out_ref, kv_ref, kt_ref, acc_ref, mine_ref, theirs_ref,
):
    block_count, slot_count = blocks_ref.shape
    half = block_count // 2
    zero = jnp.zeros((BLOCK, HEAD_DIM), BF16)

    def prepare(c, carry):
        k_one, v_one = qkv_ref[c, KEY], qkv_ref[c, VALUE]
        kv_ref[rows_of(c), :] = jnp.concatenate([k_one, v_one], axis=1)
        kt_ref[c] = k_one.T
        acc_ref[rows_of(c), :] = jnp.zeros((BLOCK, 2 * HEAD_DIM), F32)
        return carry

    lax.fori_loop(0, block_count, prepare, 0, unroll=2)
    first = early_ref.shape[0]
    mine_ref[:first] = early_ref[...]
    mine_ref[first:] = late_ref[...]
    theirs_ref[:first] = theirs_early_ref[...]
    theirs_ref[first:] = theirs_late_ref[...]

    def one(b, d_one):
        q_one = qkv_ref[b, QUERY]
        q_t, d_t = q_one.T, d_one.T
        owners = [blocks_ref[b, s] for s in range(slot_count)]
        right = jnp.concatenate(
            [jnp.concatenate([q_t, zero], axis=1), jnp.concatenate([zero, d_t], axis=1)], axis=0
        )
        lse = lse_ref[b]
        row_dot = jnp.sum(attn_t_ref[b].astype(F32) * d_t.astype(F32), axis=0, keepdims=True)
        pairs = []
        for c in owners:
            both = jnp.dot(kv_ref[rows_of(c), :], right, preferred_element_type=F32)
            prob = jnp.exp2(both[:, :BLOCK] * (INV_ROOT * LOG2E) - lse)
            score_grad = (prob * (both[:, BLOCK:] - row_dot) * INV_ROOT).astype(BF16)
            pairs.append((score_grad, prob.astype(BF16)))
        back = jnp.concatenate(
            [jnp.concatenate([q_one, zero], axis=1), jnp.concatenate([zero, d_one], axis=1)], axis=0
        )
        for c, pair in zip(owners, pairs):
            acc_ref[rows_of(c), :] += jnp.dot(
                jnp.concatenate(pair, axis=1), back, preferred_element_type=F32
            )
        k_t = jnp.concatenate([kt_ref[c] for c in owners], axis=1)
        score_grads = jnp.concatenate([score_grad for score_grad, _ in pairs], axis=0)
        dq_t = jnp.dot(k_t, score_grads, preferred_element_type=F32)
        out_ref[b, 0] = dq_t.astype(BF16).T

    def step(i, carry):
        chip = lax.rem(place_ref[0] + place_ref[2 + i], half)
        one(2 * chip + place_ref[1], mine_ref[i])
        one(2 * chip + 1 - place_ref[1], theirs_ref[i])
        return carry

    lax.fori_loop(0, half, step, 0)

    def finish(c, carry):
        out_ref[c, 1] = acc_ref[rows_of(c), :HEAD_DIM].astype(BF16)
        out_ref[c, 2] = acc_ref[rows_of(c), HEAD_DIM:].astype(BF16)
        return carry

    lax.fori_loop(0, block_count, finish, 0, unroll=2)


def backward(blocks, place, qkv, attn_t, lse, *attn_grads):
    count = qkv.shape[0]
    return pl.pallas_call(
        backward_kernel,
        out_shape=like(count, 3, BLOCK, HEAD_DIM),
        in_specs=[SM, SM] + [VM] * (3 + len(attn_grads)),
        out_specs=VM,
        scratch_shapes=[
            pltpu.VMEM((count * BLOCK, 2 * HEAD_DIM), BF16),
            pltpu.VMEM((count, HEAD_DIM, BLOCK), BF16),
            pltpu.VMEM((count * BLOCK, 2 * HEAD_DIM), F32),
            pltpu.VMEM((count // 2, BLOCK, HEAD_DIM), BF16),
            pltpu.VMEM((count // 2, BLOCK, HEAD_DIM), BF16),
        ],
        compiler_params=pltpu.CompilerParams(vmem_limit_bytes=24 * MIB),
        cost_estimate=cost(13 * MICROSECOND),
        name="backward",
    )(blocks, place, qkv, attn_t, lse, *attn_grads)


def project_kernel(pieces, cols_ref, core_ref, mine_ref, *refs):
    own_refs, other_refs = refs[: len(pieces)], refs[len(pieces) : 2 * len(pieces)]
    layer_ref, rows_buf = refs[2 * len(pieces) :]
    count = mine_ref.shape[0]
    for h in range(count):
        rows_buf[:, h * HEAD_DIM : (h + 1) * HEAD_DIM] = mine_ref[h]
    rows = rows_buf[...]
    lower = core_ref[0] == 0
    groups = max(high for _, _, high in pieces)
    for n, (shift, low, high) in enumerate(pieces):
        for j in range(0, high - low, 2):
            weights = []
            for t in (j, j + 1):
                own, other = own_refs[n][t], other_refs[n][t]
                first = jnp.where(lower, own, other)
                second = jnp.where(lower, other, own)
                weights.append(
                    jnp.concatenate([first, second], axis=1).reshape(count * HEAD_DIM, BLOCK)
                )
            found = jnp.dot(
                rows, jnp.concatenate(weights, axis=1), preferred_element_type=F32
            ).astype(BF16)
            for t in range(2):
                at = pl.multiple_of(cols_ref[shift * groups + low + j + t] * BLOCK, BLOCK)
                layer_ref[:, pl.ds(at, BLOCK)] = found[:, t * BLOCK : (t + 1) * BLOCK]


def project(pieces, cols, core, mine, own, other):
    count = mine.shape[0]
    return pl.pallas_call(
        functools.partial(project_kernel, pieces),
        out_shape=like(BLOCK, cols.shape[0] * BLOCK),
        in_specs=[SM, SM] + [VM] * (1 + 2 * len(pieces)),
        out_specs=VM,
        scratch_shapes=[pltpu.VMEM((BLOCK, count * HEAD_DIM), BF16)],
        compiler_params=pltpu.CompilerParams(vmem_limit_bytes=32 * MIB),
        cost_estimate=cost(6 * MICROSECOND),
        name="project",
    )(cols, core, mine, *(in_hbm(w) for w in own + other))


def unpack_kernel(grads_ref, dq_ref, dk_ref, dv_ref):
    for h in range(grads_ref.shape[0]):
        cols = slice(h * HEAD_DIM, (h + 1) * HEAD_DIM)
        dq_ref[:, cols] = grads_ref[h, 0]
        dk_ref[:, cols] = grads_ref[h, 1]
        dv_ref[:, cols] = grads_ref[h, 2]


def unpack(grads):
    wide = like(BLOCK, grads.shape[0] * HEAD_DIM)
    return pl.pallas_call(
        unpack_kernel,
        out_shape=(wide, wide, wide),
        in_specs=[VM],
        out_specs=(VM,) * 3,
        compiler_params=pltpu.CompilerParams(vmem_limit_bytes=24 * MIB),
        cost_estimate=cost(2 * MICROSECOND),
        name="unpack",
    )(grads)


def assemble_kernel(places_ref, *refs):
    part_refs, pg_ref = refs[:-1], refs[-1]
    wide = part_refs[0].shape[0] * BLOCK
    for i, part_ref in enumerate(part_refs):
        for t in range(part_ref.shape[0]):
            at = pl.ds(pl.multiple_of(places_ref[i] * wide + t * BLOCK, BLOCK), BLOCK)
            pg_ref[:, at] = part_ref[t].astype(F32)


def assemble(places, parts):
    groups = len(parts)
    return pl.pallas_call(
        assemble_kernel,
        out_shape=like(HEAD_DIM, groups * parts[0].shape[0] * BLOCK, dtype=F32),
        in_specs=[SM] + [VM] * groups,
        out_specs=VM,
        compiler_params=pltpu.CompilerParams(vmem_limit_bytes=24 * MIB),
        cost_estimate=cost(MICROSECOND),
        name="assemble",
    )(places, *parts)


def shifted(value, axis, by):
    size = lax.axis_size(axis)
    return lax.ppermute(value, axis, [(i, (i + by) % size) for i in range(size)])


def from_others(value, axis):
    return [value] + [shifted(value, axis, i) for i in range(1, lax.axis_size(axis))]


def exchanged(value, axis):
    size = lax.axis_size(axis)
    here = lax.axis_index(axis)
    pieces = [
        lax.dynamic_index_in_dim(value, (here + i) % size, 0, keepdims=False) for i in range(size)
    ]
    return pieces[:1] + [shifted(piece, axis, i) for i, piece in enumerate(pieces) if i]


def total_of(pieces):
    return sum(piece.astype(F32) for piece in pieces)


def swapped(value):
    return lax.ppermute(value, "c", [(0, 1), (1, 0)])


def body(query_in, key_in, value_in, out_grad, out_proj, key_blocks):
    seq, dp = ("z", "c"), ("x", "y")
    chips = lax.axis_size("z")
    core, z = lax.axis_index("c").astype(jnp.int32), lax.axis_index("z").astype(jnp.int32)
    x, y = lax.axis_index("x").astype(jnp.int32), lax.axis_index("y").astype(jnp.int32)
    tokens = lax.axis_size(seq) * lax.axis_size(dp) * query_in.shape[1]
    groups = lax.axis_size("x")
    chunks = out_proj.shape[1] // BLOCK
    blocks = key_blocks[0]
    index = jnp.arange(groups, dtype=jnp.int32)

    place = (x * groups + y)[None]
    qkv_out, gw = pack(place, query_in[0], key_in[0], value_in[0], out_grad[0], out_proj)
    qkv = lax.all_to_all(qkv_out, seq, split_axis=0, concat_axis=0, tiled=True)
    proj_theirs = swapped(out_proj)

    shifts, parts, shards = [0], [(0, 0, chunks)], [gw]
    up = down = gw
    for k in range(1, chips // 2):
        if k == 2:
            qkv, up, down = lax.optimization_barrier((qkv, up, down))
            w_near = from_others(qkv[:, 3 * BLOCK :], "y")
        if k == 3:
            up, down, w_near = lax.optimization_barrier((up, down, w_near))
            w_here = jnp.stack(w_near)
            w_up, w_down = shifted(w_here, "x", 1), shifted(w_here, "x", -1)
        up, down = shifted(up, "z", 1), shifted(down, "z", -1)
        for shift, array in ((-k, up), (k, down)):
            parts.append((len(shifts), 0, chunks))
            shifts.append(shift)
            shards.append(array)
    cut = chunks // 2
    attn, attn_t, lse = forward(blocks, qkv)
    attn, up, down = lax.optimization_barrier((attn, up, down))
    shards += [shifted(up[:cut], "z", 1), shifted(down[cut:], "z", -1)]
    parts += [(len(shifts), 0, cut), (len(shifts), cut, chunks)]
    shifts.append(chips // 2)
    parts = tuple(parts)
    steps = jnp.array([s % chips for s in shifts], jnp.int32)
    spot = jnp.concatenate([jnp.stack([z, core]), steps])

    other_t = swapped(
        lax.dynamic_index_in_dim(
            attn_t.reshape((chips, 2) + attn_t.shape[1:]), 1 - core, 1, keepdims=False
        )
    )
    early, theirs_early = attn_grad(parts[:-2], out_proj, proj_theirs, shards[:-2])
    theirs_early = swapped(theirs_early)
    attn, early, shards[-2], shards[-1], w_up, w_down = lax.optimization_barrier(
        (attn, early, shards[-2], shards[-1], w_up, w_down)
    )
    attn_rows = lax.all_to_all(attn, seq, split_axis=0, concat_axis=0, tiled=True)
    late, theirs_late = attn_grad(
        ((0, 0, cut), (0, cut, chunks)), out_proj, proj_theirs, shards[-2:]
    )
    theirs_late = swapped(theirs_late)
    w_far = shifted(w_up, "x", 1)
    grads = backward(blocks, spot, qkv, attn_t, lse, early, theirs_early, late, theirs_late)
    grads, attn_rows, other_t = lax.optimization_barrier((grads, attn_rows, other_t))
    grad_rows = lax.all_to_all(grads, seq, split_axis=0, concat_axis=0, tiled=True)

    pg_mine, pg_theirs = weight_grad(parts, spot, attn_t, other_t, chunks, shards)
    pg_theirs, w_far = lax.optimization_barrier((pg_theirs, w_far))
    pg = (pg_mine.astype(F32) + swapped(pg_theirs).astype(F32)).astype(BF16)
    pg_pieces = exchanged(pg.reshape((groups, groups) + pg.shape[1:]), "x")
    pieces = tuple((i, 0, groups) for i in (0, 1, groups - 1, 2))
    weights = [w_here, w_up, w_down, w_far]
    cols = (((x - index) % groups)[:, None] * groups + ((y - index) % groups)[None]).reshape(-1)
    layer = project(pieces, cols, core[None], attn_rows, weights, [swapped(w) for w in weights])
    pg_pieces, layer = lax.optimization_barrier((pg_pieces, layer))
    pg = total_of(from_others(total_of(pg_pieces).astype(BF16), "y"))
    pg = (pg * (1.0 / math.sqrt(tokens))).astype(BF16)
    pg_pieces = from_others(pg, "x")
    dq, dk, dv = unpack(grad_rows)
    pg_pieces, dq, dk, dv = lax.optimization_barrier((pg_pieces, dq, dk, dv))
    proj_grad = assemble((x - index) % groups, pg_pieces)
    return layer[None], dq[None], dk[None], dv[None], proj_grad


def solution(mesh):
    split = Mesh(mesh.devices.reshape(8, 2, 4, 4), ("z", "c", "x", "y"))
    rows = P(("x", "y"), ("z", "c"), None)
    in_specs = (rows, rows, rows, rows, P(("z", "c"), None), P(("z", "c"), None, None))
    out_specs = (rows, rows, rows, rows, P(("z", "c"), None))
    return jax.shard_map(body, mesh=split, in_specs=in_specs, out_specs=out_specs, check_vma=False)
```
